512 devices in a mesh: tm: 64 (over x, y, core), dp: 8 (over z).
Axes of the slice: x: 4, y: 8, z: 8, core: 2. Of those that a mesh axis runs over, the one named last changes fastest.
Arguments:
- frame_tokens: bfloat16 [8, 192, 64, 1280], P('dp', 'tm'), may hold values from -8 to 8
- visible: int32 [8, 192, 64], P('dp'), may hold values from 0 to 2
- grad_output: bfloat16 [8, 192, 64, 1280], P('dp', 'tm'), may hold values from -16 to 16
- norm_gain: float32 [1280], replicated, may hold values from 0.1 to 1.9
- query_weight: bfloat16 [1280, 640], P('tm'), may hold values from -1.5 to 1.5
- key_weight: bfloat16 [1280, 640], P('tm'), may hold values from -1.5 to 1.5
- value_weight: bfloat16 [1280, 640], P('tm'), may hold values from -0.15625 to 0.15625
- output_weight: bfloat16 [640, 1280], P('tm'), may hold values from -0.25 to 0.25
Outputs:
- block_out: bfloat16 [8, 192, 64, 1280], P('dp', 'tm')
- grad_tokens: bfloat16 [8, 192, 64, 1280], P('dp', 'tm')
- grad_output_weight: float32 [640, 1280], P('tm')
The draws below stay inside these ranges and needn't reach their ends.
Inputs may be any that keep to these rules, and one draw needn't show every extreme that they name: visible[c, f, g] names which of the 3 cells of group g is visible in frame f.
All inputs are finite; a program needn't handle non-finite values.
Results may differ from the reference program's by a relative error of at most 0.012.
Values may be sent and summed in bfloat16 or wider, within the bound.
No kernel may reach another device: no remote copies, remote signals or barrier semaphores. Data moves between devices by JAX's collectives and lax.ppermute only.
A program may use at most 64 MiB of HBM per device.

```python
import math
import jax
import jax.numpy as jnp
from jax import lax

D = 1280
HEADS = 8
HEAD_DIM = 80
ATT = 640
VIS = 64
GROUP_CELLS = 3
FRAMES = 192
CLIPS = 8


def draw_frame_tokens(key, part):
    noise = jax.random.normal(jax.random.fold_in(key, 31), (CLIPS, FRAMES, VIS, D), jnp.float32)
    return jnp.clip(noise, -7.5, 7.5).astype(jnp.bfloat16)


def query_key_pair(key):
    first = jax.random.normal(jax.random.fold_in(key, 41), (D, HEADS * HEAD_DIM), jnp.float32) / math.sqrt(D)
    second = jax.random.normal(jax.random.fold_in(key, 42), (D, HEADS * HEAD_DIM), jnp.float32) / math.sqrt(D)
    return (jnp.clip(first, -1.5, 1.5), jnp.clip(second, -1.5, 1.5))


def draw_query_weight(key, part):
    return query_key_pair(key)[0].astype(jnp.bfloat16)


def draw_key_weight(key, part):
    return query_key_pair(key)[1].astype(jnp.bfloat16)


def set_ends(array, rng, least, largest):
    shape = array.shape
    place = [jax.random.randint(jax.random.fold_in(rng, axis), (), 0, shape[axis]) for axis in range(len(shape))]
    array = array.at[tuple(place)].set(least)
    longest = shape.index(max(shape))
    place[longest] = (place[longest] + 1) % shape[longest]
    return array.at[tuple(place)].set(largest)


def with_spikes(values, key, source, target, parts, factor):
    def block_of(dim):
        return (jnp.arange(values.shape[dim]) // (values.shape[dim] // parts)).reshape((-1,) + (1,) * (values.ndim - 1 - dim))

    near = jax.random.permutation(key, parts)[block_of(target)]
    far = (block_of(target) + parts // 2) % parts
    return jnp.where((block_of(source) == near) | (block_of(source) == far), factor * values, values)


def level_of(own_key, dims, cuts, least, high):
    level = 1.0
    for axis_at, shards_of in cuts:
        steps = jax.random.uniform(jax.random.fold_in(jax.random.fold_in(own_key, 6), axis_at), (shards_of,), jnp.float32, least / len(cuts), high / len(cuts))
        level = level * jnp.repeat(jnp.exp(steps), dims[axis_at] // shards_of).reshape((-1,) + (1,) * (len(dims) - 1 - axis_at))
    return level


def gaussian(stream_key, extent, scale, most, pieces=(), held_as=jnp.bfloat16):
    values = jax.random.normal(stream_key, extent, jnp.float32) * scale
    if len(pieces) > 0:
        values = level_of(stream_key, extent, pieces, -0.22, 0.18) * values
    return jnp.clip(values, min=-most, max=most).astype(held_as)


def bell_draw_with(own_key, shape, scale, bound, pieces, heavy, kind=jnp.bfloat16):
    array = scale * jax.random.normal(own_key, shape, jnp.float32)
    if pieces:
        array = array * level_of(own_key, shape, pieces, -0.22, 0.18)
    return jnp.clip(with_spikes(array, jax.random.fold_in(own_key, 3), *heavy), -bound, bound).astype(kind)


def setup_inputs(seed: int = 0) -> dict:
    arg_keys = jax.random.split(jax.random.key(seed), 9)
    return {
        "frame_tokens": draw_frame_tokens(jax.random.fold_in(arg_keys[8], 71), 0),
        "visible": set_ends(jax.random.randint(arg_keys[1], (CLIPS, FRAMES, VIS), 0, GROUP_CELLS), jax.random.fold_in(arg_keys[1], 1), 0, GROUP_CELLS - 1).astype(jnp.int32),
        "grad_output": bell_draw_with(arg_keys[2], (CLIPS, FRAMES, VIS, D), 1.0, 16.0, ((0, 8), (1, 64)), (1, 3, 64, 4.0)),
        "norm_gain": jnp.clip(1.0 + 0.18 * jax.random.normal(arg_keys[3], (D,), jnp.float32), 0.1, 1.9),
        "query_weight": draw_query_weight(jax.random.fold_in(arg_keys[8], 71), 0),
        "key_weight": draw_key_weight(jax.random.fold_in(arg_keys[8], 71), 0),
        "value_weight": gaussian(arg_keys[6], (D, ATT), D ** -0.5, 0.15625, ((0, 64),)),
        "output_weight": gaussian(arg_keys[7], (ATT, D), ATT ** -0.5, 0.25, ((0, 64),)),
    }


NORM_EPS = 1e-06

def normalize(token_rows, norm_gain):
    values = token_rows.astype(jnp.float32)
    centered = values - lax.optimization_barrier(jnp.mean(values, axis=-1, keepdims=True))
    inverse = lax.rsqrt(lax.optimization_barrier(jnp.mean(centered * centered, axis=-1, keepdims=True)) + NORM_EPS)
    scaled = centered * inverse
    return (scaled, inverse, (scaled * norm_gain).astype(jnp.bfloat16))

def project(token_rows, weight):
    lead_shape = token_rows.shape[:-1]
    flat_rows = token_rows.reshape(-1, token_rows.shape[-1])
    result = jnp.dot(flat_rows, weight, preferred_element_type=jnp.float32)
    return result.astype(jnp.bfloat16).reshape(lead_shape + (weight.shape[1],))

def split_heads(values):
    return values.reshape(values.shape[:-1] + (HEADS, values.shape[-1] // HEADS)).astype(jnp.float32)

def attend(query_rows, key_rows, value_rows, same_cell):
    score_scale = 1.0 / jnp.sqrt(jnp.float32(HEAD_DIM))
    query_heads = split_heads(query_rows)
    key_heads = split_heads(key_rows)
    value_heads = split_heads(value_rows)
    scores = jnp.einsum('fghe,tghe->ghft', query_heads, key_heads) * score_scale
    scores = jnp.where(same_cell[:, None], scores, -jnp.inf)
    row_top = lax.optimization_barrier(jnp.max(scores, axis=-1, keepdims=True))
    expons = jnp.exp(scores - row_top)
    soft_probs = expons / lax.optimization_barrier(jnp.sum(expons, axis=-1, keepdims=True))
    probs_low = soft_probs.astype(jnp.bfloat16)
    mixed_rows = jnp.einsum('ghft,tghe->fghe', probs_low.astype(jnp.float32), value_heads)
    return (soft_probs, probs_low, mixed_rows.reshape(query_rows.shape).astype(jnp.bfloat16))

def attend_back(query_rows, key_rows, value_rows, soft_probs, probs_low, grad_mixed):
    score_scale = 1.0 / jnp.sqrt(jnp.float32(HEAD_DIM))
    query_heads = split_heads(query_rows)
    key_heads = split_heads(key_rows)
    value_heads = split_heads(value_rows)
    grad_heads = split_heads(grad_mixed)
    grad_probs = jnp.einsum('fghe,tghe->ghft', grad_heads, value_heads)
    centre = lax.optimization_barrier(jnp.sum(soft_probs * grad_probs, axis=-1, keepdims=True))
    grad_scores = (soft_probs * (grad_probs - centre) * score_scale).astype(jnp.bfloat16).astype(jnp.float32)
    grad_query = jnp.einsum('ghft,tghe->fghe', grad_scores, key_heads)
    grad_key = jnp.einsum('ghft,fghe->tghe', grad_scores, query_heads)
    grad_value = jnp.einsum('ghft,fghe->tghe', probs_low.astype(jnp.float32), grad_heads)
    full_shape = query_rows.shape
    return (grad_query.reshape(full_shape).astype(jnp.bfloat16), grad_key.reshape(full_shape).astype(jnp.bfloat16), grad_value.reshape(full_shape).astype(jnp.bfloat16))

def back_project(grad_query, grad_key, grad_value, query_weight, key_weight, value_weight):
    lead_shape = grad_query.shape[:-1]
    width = grad_query.shape[-1]
    total = jnp.dot(grad_query.reshape(-1, width), query_weight.T, preferred_element_type=jnp.float32)
    total = total + jnp.dot(grad_key.reshape(-1, width), key_weight.T, preferred_element_type=jnp.float32)
    total = total + jnp.dot(grad_value.reshape(-1, width), value_weight.T, preferred_element_type=jnp.float32)
    return total.astype(jnp.bfloat16).reshape(lead_shape + (query_weight.shape[0],))

def reference(frame_tokens, visible, grad_output, norm_gain, query_weight, key_weight, value_weight, output_weight):

    def one_clip(inputs):
        tokens, cells, grad_clip = inputs
        scaled, inverse, normed = normalize(tokens, norm_gain)
        query_rows = project(normed, query_weight)
        key_rows = project(normed, key_weight)
        value_rows = project(normed, value_weight)
        cell_major = cells.T
        same_cell = cell_major[:, :, None] == cell_major[:, None, :]
        soft_probs, probs_low, mixed_rows = attend(query_rows, key_rows, value_rows, same_cell)
        flat_mixed = mixed_rows.reshape(-1, mixed_rows.shape[-1])
        flat_tokens = tokens.reshape(-1, tokens.shape[-1])
        update = jnp.dot(flat_mixed, output_weight, preferred_element_type=jnp.float32)
        block_rows = (flat_tokens.astype(jnp.float32) + update).astype(jnp.bfloat16).reshape(tokens.shape)
        flat_grad = grad_clip.reshape(-1, grad_clip.shape[-1])
        grad_mixed = jnp.dot(flat_grad, output_weight.T, preferred_element_type=jnp.float32)
        grad_mixed = grad_mixed.astype(jnp.bfloat16).reshape(mixed_rows.shape)
        weight_term = jnp.dot(flat_mixed.T, flat_grad, preferred_element_type=jnp.float32)
        grad_query, grad_key, grad_value = attend_back(query_rows, key_rows, value_rows, soft_probs, probs_low, grad_mixed)
        grad_normed = back_project(grad_query, grad_key, grad_value, query_weight, key_weight, value_weight)
        weighted = grad_normed.astype(jnp.float32) * norm_gain
        first_mean = lax.optimization_barrier(jnp.mean(weighted, axis=-1, keepdims=True))
        second_mean = lax.optimization_barrier(jnp.mean(weighted * scaled, axis=-1, keepdims=True))
        grad_rows = inverse * (weighted - first_mean - scaled * second_mean) + grad_clip.astype(jnp.float32)
        return (block_rows, grad_rows.astype(jnp.bfloat16), weight_term)
    block_out, grad_tokens, weight_terms = lax.map(one_clip, (frame_tokens, visible, grad_output))
    return (block_out, grad_tokens, lax.optimization_barrier(jnp.sum(weight_terms, axis=0)))
```

```python
import functools
import math

import jax
import jax.numpy as jnp
from jax import lax
from jax.experimental import pallas as pl
from jax.experimental.pallas import tpu as pltpu
from jax.sharding import Mesh
from jax.sharding import PartitionSpec as P

HEADS = 8
NORM_EPS = 1e-06
PARTS = ("x", "y", "core")
SIZES = (4, 8, 2)


def dot(left, right, contract):
    return lax.dot_general(
        left, right, (contract, ((), ())), preferred_element_type=jnp.float32
    )


NN = ((1,), (0,))
NT = ((1,), (1,))
TN = ((0,), (0,))


def cell_kernel(normed_ref, grad_ref, row_ref, col_ref, qkv_ref, out_ref,
                mixed_ref, normed_grad_ref, weight_ref):
    low = jnp.bfloat16
    att = out_ref.shape[0]
    size = att // HEADS
    scale = 1.0 / math.sqrt(size)
    qkv = dot(normed_ref[...], qkv_ref[...], NN).astype(low)
    grad_mixed = dot(grad_ref[...], out_ref[...], NT).astype(low)
    same = row_ref[...] == col_ref[...]
    mixed, grad_q, grad_k, grad_v = [], [], [], []
    for h in range(HEADS):
        q = qkv[:, h * size:(h + 1) * size]
        k = qkv[:, att + h * size:att + (h + 1) * size]
        v = qkv[:, 2 * att + h * size:2 * att + (h + 1) * size]
        g = grad_mixed[:, h * size:(h + 1) * size]
        scores = jnp.where(same, dot(q, k, NT) * scale, -jnp.inf)
        expons = jnp.exp(scores - jnp.max(scores, axis=-1, keepdims=True))
        probs = expons / jnp.sum(expons, axis=-1, keepdims=True)
        probs_low = probs.astype(low)
        mixed.append(dot(probs_low, v, NN).astype(low))
        grad_probs = dot(g, v, NT)
        centre = jnp.sum(probs * grad_probs, axis=-1, keepdims=True)
        grad_scores = (probs * (grad_probs - centre) * scale).astype(low)
        grad_q.append(dot(grad_scores, k, NN).astype(low))
        grad_k.append(dot(grad_scores, q, TN).astype(low))
        grad_v.append(dot(probs_low, g, TN).astype(low))
    mixed = jnp.concatenate(mixed, axis=1)
    mixed_ref[...] = mixed
    grads = jnp.concatenate(grad_q + grad_k + grad_v, axis=1)
    normed_grad_ref[...] = dot(grads, qkv_ref[...], NT).astype(low)
    weight_ref[...] = dot(mixed, grad_ref[...], TN).astype(low)


def cell_part(normed, grad, cells, qkv_weight, output_weight, interpret=False):
    rows, width = normed.shape
    att = output_weight.shape[0]
    low = jnp.bfloat16
    return pl.pallas_call(
        cell_kernel,
        out_shape=(
            jax.ShapeDtypeStruct((rows, att), low),
            jax.ShapeDtypeStruct((rows, width), low),
            jax.ShapeDtypeStruct((att, width), low),
        ),
        compiler_params=pltpu.CompilerParams(vmem_limit_bytes=48 << 20),
        interpret=interpret,
    )(normed, grad, cells[:, None], cells[None, :], qkv_weight, output_weight)


def exchange(values, axis):
    return lax.all_to_all(values, axis, split_axis=0, concat_axis=0, tiled=True)


def add_up(parts):
    return jnp.sum(parts.astype(jnp.float32), axis=0)


def on_device(frame_tokens, visible, grad_output, norm_gain,
              query_weight, key_weight, value_weight, output_weight):
    low = jnp.bfloat16
    shards = SIZES[0] * SIZES[1] * SIZES[2]
    tokens = frame_tokens[0]
    frames, groups, width = tokens.shape
    att = query_weight.shape[1]
    depth = query_weight.shape[0]
    me = lax.axis_index(PARTS)

    share = jnp.concatenate(
        [query_weight, key_weight, value_weight, output_weight.reshape(depth, att)], axis=1
    )
    whole = lax.all_gather(share, PARTS, axis=0, tiled=False)
    qkv_weight = whole[:, :, :3 * att].reshape(width, 3 * att)
    whole_out = whole[:, :, 3 * att:].reshape(att, width)

    values = tokens.astype(jnp.float32)
    centered = values - jnp.mean(values, axis=-1, keepdims=True)
    inverse = lax.rsqrt(jnp.mean(centered * centered, axis=-1, keepdims=True) + NORM_EPS)
    scaled = centered * inverse
    normed = (scaled * norm_gain).astype(low)

    def to_cells(rows):
        sent = rows.transpose(1, 0, 2).reshape(shards, 2, -1)
        return exchange(sent, PARTS).reshape(shards * frames, -1)

    def to_frames(rows):
        sent = rows.reshape(shards, 2, -1)
        return exchange(sent, PARTS).reshape(shards, frames, -1).transpose(1, 0, 2)

    normed_cells = to_cells(normed)
    grad_cells = to_cells(grad_output[0])
    cells = lax.dynamic_slice_in_dim(visible[0], me, 1, 1)[:, 0]
    mixed_cells, grad_normed_cells, weight_part = cell_part(
        normed_cells, grad_cells, cells, qkv_weight, whole_out
    )
    mixed = to_frames(mixed_cells)
    grad_normed = to_frames(grad_normed_cells)

    halves = weight_part.reshape(att, 2, width // 2).transpose(1, 0, 2)
    part = add_up(exchange(halves, "core")).astype(low)
    part = add_up(exchange(part.reshape(SIZES[0], -1, width // 2), "x")).astype(low)
    part = add_up(exchange(part.reshape(SIZES[1], -1, width // 2), "y")).astype(low)
    part = add_up(exchange(jnp.broadcast_to(part[None], (8,) + part.shape), "dp"))
    part = exchange(part.reshape(2, -1, width // 2), "core")
    grad_weight = part.transpose(1, 0, 2).reshape(-1, width)

    flat_mixed = mixed.reshape(-1, att)
    update = jnp.dot(flat_mixed, whole_out, preferred_element_type=jnp.float32)
    block_rows = (values.reshape(-1, width) + update).astype(low).reshape(tokens.shape)
    weighted = grad_normed.astype(jnp.float32) * norm_gain
    first_mean = jnp.mean(weighted, axis=-1, keepdims=True)
    second_mean = jnp.mean(weighted * scaled, axis=-1, keepdims=True)
    grad_rows = inverse * (weighted - first_mean - scaled * second_mean)
    grad_rows = grad_rows + grad_output[0].astype(jnp.float32)
    return (block_rows[None], grad_rows.astype(low)[None], grad_weight)


def solution(mesh):
    fine = Mesh(mesh.devices.reshape(SIZES + (mesh.shape["dp"],)), PARTS + ("dp",))
    rows = P("dp", PARTS, None, None)
    weight = P(PARTS, None)
    return jax.shard_map(
        on_device,
        mesh=fine,
        in_specs=(rows, P("dp", None, None), rows, P(), weight, weight, weight, weight),
        out_specs=(rows, rows, weight),
        check_vma=False,
    )
```

```python
import math

import jax
import jax.numpy as jnp
from jax import lax
from jax.experimental import pallas as pl
from jax.experimental.pallas import tpu as pltpu
from jax.sharding import Mesh
from jax.sharding import PartitionSpec as P

HEADS = 8
NORM_EPS = 1e-06
PARTS = ("x", "y", "core")
SIZES = (4, 8, 2)


def dot(left, right, contract):
    return lax.dot_general(
        left, right, (contract, ((), ())), preferred_element_type=jnp.float32
    )


NN = ((1,), (0,))
NT = ((1,), (1,))
TN = ((0,), (0,))


def cell_kernel(normed_ref, grad_ref, row_ref, col_ref, whole_ref, pick_ref,
                mixed_ref, normed_grad_ref, own_ref, other_ref, out_ref, qkv_ref):
    low = jnp.bfloat16
    shards, depth, _ = whole_ref.shape
    att, width = out_ref.shape
    size = att // HEADS
    half = depth // 2
    scale = 1.0 / math.sqrt(size)
    for d in range(shards):
        qkv_ref[d * depth:(d + 1) * depth, :] = whole_ref[d, :, :3 * att]
        out_ref[d * half:(d + 1) * half, :width // 2] = whole_ref[d, :half, 3 * att:]
        out_ref[d * half:(d + 1) * half, width // 2:] = whole_ref[d, half:, 3 * att:]
    qkv = dot(normed_ref[...], qkv_ref[...], NN).astype(low)
    grad_mixed = dot(grad_ref[...], out_ref[...], NT).astype(low)
    same = row_ref[...] == col_ref[...]
    mixed, grad_q, grad_k, grad_v = [], [], [], []
    for h in range(HEADS):
        q = qkv[:, h * size:(h + 1) * size]
        k = qkv[:, att + h * size:att + (h + 1) * size]
        v = qkv[:, 2 * att + h * size:2 * att + (h + 1) * size]
        g = grad_mixed[:, h * size:(h + 1) * size]
        scores = jnp.where(same, dot(q, k, NT) * scale, -jnp.inf)
        expons = jnp.exp(scores - jnp.max(scores, axis=-1, keepdims=True))
        probs = expons / jnp.sum(expons, axis=-1, keepdims=True)
        probs_low = probs.astype(low)
        mixed.append(dot(probs_low, v, NN).astype(low))
        grad_probs = dot(g, v, NT)
        centre = jnp.sum(probs * grad_probs, axis=-1, keepdims=True)
        grad_scores = (probs * (grad_probs - centre) * scale).astype(low)
        grad_q.append(dot(grad_scores, k, NN).astype(low))
        grad_k.append(dot(grad_scores, q, TN).astype(low))
        grad_v.append(dot(probs_low, g, TN).astype(low))
    mixed = jnp.concatenate(mixed, axis=1)
    mixed_ref[...] = mixed
    own_ref[...] = dot(mixed, pick_ref[0], NN).astype(low)
    other_ref[...] = dot(mixed, pick_ref[1], NN).astype(low)
    grads = jnp.concatenate(grad_q + grad_k + grad_v, axis=1)
    normed_grad_ref[...] = dot(grads, qkv_ref[...], NT).astype(low)


def cell_part(normed, grad, cells, whole, pick, interpret=False):
    rows, width = normed.shape
    att = pick.shape[1]
    low = jnp.bfloat16
    return pl.pallas_call(
        cell_kernel,
        out_shape=(
            jax.ShapeDtypeStruct((rows, att), low),
            jax.ShapeDtypeStruct((rows, width), low),
            jax.ShapeDtypeStruct((rows, att // 2), low),
            jax.ShapeDtypeStruct((rows, att // 2), low),
            jax.ShapeDtypeStruct((att, width), low),
        ),
        scratch_shapes=[pltpu.VMEM((width, 3 * att), low)],
        compiler_params=pltpu.CompilerParams(vmem_limit_bytes=56 << 20),
        interpret=interpret,
    )(normed, grad, cells[:, None], cells[None, :], whole, pick)


def weight_kernel(place_ref, own_ref, got_ref, grad_ref, got_grad_ref, *rest):
    outs, total = rest[:-1], rest[-1]
    total[...] = dot(own_ref[...], grad_ref[...], TN) + dot(
        got_ref[...], got_grad_ref[...], TN
    )
    rows = total.shape[0] // len(outs)
    for k, out in enumerate(outs):
        start = pl.multiple_of(rows * lax.rem(place_ref[0] + k, len(outs)), rows)
        out[...] = total[pl.ds(start, rows), :].astype(out.dtype)


def weight_part(place, own, got, grad, got_grad, interpret=False):
    count = SIZES[0]
    rows, width = own.shape[1] // count, grad.shape[1]
    return pl.pallas_call(
        weight_kernel,
        out_shape=tuple(
            jax.ShapeDtypeStruct((rows, width), jnp.bfloat16 if k else jnp.float32)
            for k in range(count)
        ),
        in_specs=[pl.BlockSpec(memory_space=pltpu.SMEM)]
        + [pl.BlockSpec(memory_space=pltpu.VMEM)] * 4,
        scratch_shapes=[pltpu.VMEM((own.shape[1], width), jnp.float32)],
        compiler_params=pltpu.CompilerParams(vmem_limit_bytes=32 << 20),
        interpret=interpret,
    )(place, own, got, grad, got_grad)


def exchange(values, axis):
    return lax.all_to_all(values, axis, split_axis=0, concat_axis=0, tiled=True)


def shift(values, axis, step, size):
    return lax.ppermute(values, axis, [(i, (i + step) % size) for i in range(size)])


def on_device(frame_tokens, visible, grad_output, norm_gain,
              query_weight, key_weight, value_weight, output_weight):
    low = jnp.bfloat16
    clips = lax.axis_size("dp")
    shards = SIZES[0] * SIZES[1] * SIZES[2]
    tokens = frame_tokens[0]
    frames, groups, width = tokens.shape
    depth, att = query_weight.shape
    me = lax.axis_index(PARTS)
    core = lax.axis_index("core")

    folded = jnp.concatenate(
        [output_weight[:, :width // 2], output_weight[:, width // 2:]], axis=0
    )
    share = jnp.concatenate([query_weight, key_weight, value_weight, folded], axis=1)
    whole = lax.all_gather(share, PARTS, axis=0, tiled=False)

    values = tokens.astype(jnp.float32)
    centered = values - jnp.mean(values, axis=-1, keepdims=True)
    inverse = lax.rsqrt(jnp.mean(centered * centered, axis=-1, keepdims=True) + NORM_EPS)
    scaled = centered * inverse
    normed = (scaled * norm_gain).astype(low)

    def to_cells(rows):
        sent = rows.transpose(1, 0, 2).reshape(shards, 2, -1)
        return exchange(sent, PARTS).reshape(shards * frames, -1)

    normed_cells = to_cells(normed)
    grad_cells = to_cells(grad_output[0])
    grad_got = shift(grad_cells, "core", 1, 2)
    cells = lax.dynamic_slice_in_dim(visible[0], me, 1, 1)[:, 0]

    per = att // shards
    column = jnp.arange(att, dtype=jnp.int32)
    place = (column // (2 * per)) * per + column % per
    side = (column // per) % 2
    at = place[:, None] == jnp.arange(att // 2, dtype=jnp.int32)[None, :]
    pick = jnp.stack(
        [at & (side == core)[:, None], at & (side != core)[:, None]]
    ).astype(low)

    mixed_cells, grad_normed_cells, own, other, whole_out = cell_part(
        normed_cells, grad_cells, cells, whole, pick
    )
    got = shift(other, "core", 1, 2)
    sent = jnp.concatenate([mixed_cells, grad_normed_cells], axis=1)
    back = exchange(sent.reshape(shards, 2, -1), PARTS)
    rows = back.reshape(shards, frames, att + width).transpose(1, 0, 2)
    mixed, grad_normed = rows[:, :, :att], rows[:, :, att:]

    slabs = weight_part(
        lax.axis_index("x").astype(jnp.int32)[None], own, got, grad_cells, grad_got
    )
    part = slabs[0]
    for k in range(1, SIZES[0]):
        part = part + shift(slabs[k], "x", k, SIZES[0]).astype(jnp.float32)
    part, _ = lax.optimization_barrier((part.astype(low), back))
    part = part.reshape(SIZES[1] * clips, -1)
    part = jnp.sum(exchange(part, ("y", "dp")).astype(jnp.float32), axis=0)
    part = exchange(jnp.broadcast_to(part[None], (clips,) + part.shape), "dp")
    grad_weight = part.reshape(per, width)

    flat_mixed = mixed.reshape(-1, att)
    update = jnp.dot(flat_mixed, whole_out, preferred_element_type=jnp.float32)
    block_rows = (values.reshape(-1, width) + update).astype(low).reshape(tokens.shape)
    weighted = grad_normed.astype(jnp.float32) * norm_gain
    first_mean = jnp.mean(weighted, axis=-1, keepdims=True)
    second_mean = jnp.mean(weighted * scaled, axis=-1, keepdims=True)
    grad_rows = inverse * (weighted - first_mean - scaled * second_mean)
    grad_rows = grad_rows + grad_output[0].astype(jnp.float32)
    return (block_rows[None], grad_rows.astype(low)[None], grad_weight)


def solution(mesh):
    fine = Mesh(mesh.devices.reshape(SIZES + (mesh.shape["dp"],)), PARTS + ("dp",))
    rows = P("dp", PARTS, None, None)
    weight = P(PARTS, None)
    return jax.shard_map(
        on_device,
        mesh=fine,
        in_specs=(rows, P("dp", None, None), rows, P(), weight, weight, weight, weight),
        out_specs=(rows, rows, weight),
        check_vma=False,
    )
```

```python
import math

import jax
import jax.numpy as jnp
from jax import lax
from jax.experimental import pallas as pl
from jax.experimental.pallas import tpu as pltpu
from jax.sharding import Mesh
from jax.sharding import PartitionSpec as P

HEADS = 8
NORM_EPS = 1e-06
PARTS = ("x", "y", "core")
SIZES = (4, 8, 2)


def dot(left, right, contract):
    return lax.dot_general(
        left, right, (contract, ((), ())), preferred_element_type=jnp.float32
    )


NN = ((1,), (0,))
NT = ((1,), (1,))
TN = ((0,), (0,))


def cell_kernel(normed_ref, grad_ref, row_ref, col_ref, whole_ref, pick_ref,
                sent_ref, own_ref, other_ref, out_ref, qkv_ref):
    low = jnp.bfloat16
    _, lines, depth, _ = whole_ref.shape
    depth //= 2
    att, width = out_ref.shape
    size = att // HEADS
    half = depth // 2
    scale = 1.0 / math.sqrt(size)
    for d in range(SIZES[0] * SIZES[1] * SIZES[2]):
        x, y, core = d // (lines * 2), d // 2 % lines, d % 2
        piece = whole_ref.at[x * 2 + core, y]
        qkv_ref[d * depth:(d + 1) * depth, :2 * att] = piece[:depth, :]
        qkv_ref[d * depth:(d + 1) * depth, 2 * att:] = piece[depth:, :att]
        out_ref[d * half:(d + 1) * half, :att] = piece[depth:depth + half, att:]
        out_ref[d * half:(d + 1) * half, att:] = piece[depth + half:, att:]
    qkv = dot(normed_ref[...], qkv_ref[...], NN).astype(low)
    grad_mixed = dot(grad_ref[...], out_ref[...], NT).astype(low)
    same = row_ref[...] == col_ref[...]
    mixed, grad_q, grad_k, grad_v = [], [], [], []
    for h in range(HEADS):
        q = qkv[:, h * size:(h + 1) * size]
        k = qkv[:, att + h * size:att + (h + 1) * size]
        v = qkv[:, 2 * att + h * size:2 * att + (h + 1) * size]
        g = grad_mixed[:, h * size:(h + 1) * size]
        scores = jnp.where(same, dot(q, k, NT) * scale, -jnp.inf)
        expons = jnp.exp(scores - jnp.max(scores, axis=-1, keepdims=True))
        probs = expons / jnp.sum(expons, axis=-1, keepdims=True)
        probs_low = probs.astype(low)
        mixed.append(dot(probs_low, v, NN).astype(low))
        grad_probs = dot(g, v, NT)
        centre = jnp.sum(probs * grad_probs, axis=-1, keepdims=True)
        grad_scores = (probs * (grad_probs - centre) * scale).astype(low)
        grad_q.append(dot(grad_scores, k, NN).astype(low))
        grad_k.append(dot(grad_scores, q, TN).astype(low))
        grad_v.append(dot(probs_low, g, TN).astype(low))
    mixed = jnp.concatenate(mixed, axis=1)
    sent_ref[:, :att] = mixed
    own_ref[...] = dot(mixed, pick_ref[0], NN).astype(low)
    other_ref[...] = dot(mixed, pick_ref[1], NN).astype(low)
    grads = jnp.concatenate(grad_q + grad_k + grad_v, axis=1)
    sent_ref[:, att:] = dot(grads, qkv_ref[...], NT).astype(low)


def cell_part(normed, grad, cells, whole, pick, interpret=False):
    rows, width = normed.shape
    att = pick.shape[1]
    low = jnp.bfloat16
    return pl.pallas_call(
        cell_kernel,
        out_shape=(
            jax.ShapeDtypeStruct((rows, att + width), low),
            jax.ShapeDtypeStruct((rows, att // 2), low),
            jax.ShapeDtypeStruct((rows, att // 2), low),
            jax.ShapeDtypeStruct((att, width), low),
        ),
        scratch_shapes=[pltpu.VMEM((width, 3 * att), low)],
        compiler_params=pltpu.CompilerParams(vmem_limit_bytes=56 << 20),
        interpret=interpret,
    )(normed, grad, cells[:, None], cells[None, :], whole, pick)


def weight_kernel(bit_ref, own_ref, got_ref, grad_ref, got_grad_ref, stay_ref, send_ref):
    total = dot(own_ref[...], grad_ref[...], TN) + dot(got_ref[...], got_grad_ref[...], TN)
    halve(bit_ref[0], total, stay_ref, send_ref)


def fold_kernel(bit_ref, stayed_ref, got_ref, stay_ref, send_ref):
    halve(bit_ref[0], stayed_ref[...] + got_ref[...].astype(jnp.float32), stay_ref, send_ref)


def halve(bit, total, stay_ref, send_ref):
    rows = stay_ref.shape[0]
    for side in range(2):
        @pl.when(bit == side)
        def _():
            stay_ref[...] = total[side * rows:(side + 1) * rows]
            send_ref[...] = total[(1 - side) * rows:(2 - side) * rows].astype(send_ref.dtype)


def halving(body, rows, bit, *operands, interpret=False):
    width = operands[-1].shape[1]
    return pl.pallas_call(
        body,
        out_shape=(
            jax.ShapeDtypeStruct((rows, width), jnp.float32),
            jax.ShapeDtypeStruct((rows, width), jnp.bfloat16),
        ),
        in_specs=[pl.BlockSpec(memory_space=pltpu.SMEM)]
        + [pl.BlockSpec(memory_space=pltpu.VMEM)] * len(operands),
        compiler_params=pltpu.CompilerParams(vmem_limit_bytes=32 << 20),
        interpret=interpret,
    )(bit, *operands)


def exchange(values, axis):
    return lax.all_to_all(values, axis, split_axis=0, concat_axis=0, tiled=True)


def shift(values, axis, step, size):
    return lax.ppermute(values, axis, [(i, (i + step) % size) for i in range(size)])


def swap(values, axis, flip, size):
    return lax.ppermute(values, axis, [(i, i ^ flip) for i in range(size)])


def on_device(frame_tokens, visible, grad_output, norm_gain,
              query_weight, key_weight, value_weight, output_weight):
    low = jnp.bfloat16
    clips = lax.axis_size("dp")
    shards = SIZES[0] * SIZES[1] * SIZES[2]
    tokens = frame_tokens[0]
    frames, groups, width = tokens.shape
    depth, att = query_weight.shape
    me = lax.axis_index(PARTS)
    core = lax.axis_index("core")

    folded = jnp.concatenate(
        [output_weight[:, :width // 2], output_weight[:, width // 2:]], axis=0
    )
    share = jnp.concatenate(
        [
            jnp.concatenate([query_weight, key_weight], axis=1),
            jnp.concatenate([value_weight, folded], axis=1),
        ],
        axis=0,
    )
    line = exchange(jnp.broadcast_to(share[None], (SIZES[1],) + share.shape), "y")
    whole = lax.all_gather(line, ("x", "core"), axis=0, tiled=False)

    values = tokens.astype(jnp.float32)
    centered = values - jnp.mean(values, axis=-1, keepdims=True)
    inverse = lax.rsqrt(jnp.mean(centered * centered, axis=-1, keepdims=True) + NORM_EPS)
    scaled = centered * inverse
    normed = (scaled * norm_gain).astype(low)

    def to_cells(rows):
        sent = rows.transpose(1, 0, 2).reshape(shards, 2, -1)
        return exchange(sent, PARTS).reshape(shards * frames, -1)

    normed_cells = to_cells(normed)
    grad_cells = to_cells(grad_output[0])
    grad_got = shift(grad_cells, "core", 1, 2)
    cells = lax.dynamic_slice_in_dim(visible[0], me, 1, 1)[:, 0]

    per = att // shards
    column = jnp.arange(att, dtype=jnp.int32)
    x, y = column // (per * 16), column // (per * 2) % 8
    place = (x % 2) * 16 + x // 2 * 8 + (y % 2) * 4 + y // 2 % 2 * 2 + y // 4
    place = place * per + column % per
    side = column // per % 2
    at = place[:, None] == jnp.arange(att // 2, dtype=jnp.int32)[None, :]
    pick = jnp.stack(
        [at & (side == core)[:, None], at & (side != core)[:, None]]
    ).astype(low)

    sent, own, other, whole_out = cell_part(
        normed_cells, grad_cells, cells, whole, pick
    )
    got = shift(other, "core", 1, 2)
    back = exchange(sent.reshape(shards, 2, -1), PARTS)
    rows = back.reshape(shards, frames, att + width).transpose(1, 0, 2)
    mixed, grad_normed = rows[:, :, :att], rows[:, :, att:]

    steps = (("x", 0), ("x", 1), ("y", 0), ("y", 1), ("y", 2))
    count = att // 2
    stay = None
    for axis, level in steps:
        count //= 2
        bit = ((lax.axis_index(axis) >> level) & 1).astype(jnp.int32)[None]
        if stay is None:
            stay, send = halving(weight_kernel, count, bit, own, got, grad_cells, grad_got)
        else:
            stay, send = halving(fold_kernel, count, bit, stay, came)
        came = swap(send, axis, 1 << level, SIZES[PARTS.index(axis)])
    part = (stay + came.astype(jnp.float32)).astype(low)
    part, _ = lax.optimization_barrier((part, back))
    part = exchange(jnp.broadcast_to(part[None], (clips,) + part.shape), "dp")
    grad_weight = jnp.sum(part.astype(jnp.float32), axis=0)

    flat_mixed = mixed.reshape(-1, att)
    update = jnp.dot(flat_mixed, whole_out, preferred_element_type=jnp.float32)
    block_rows = (values.reshape(-1, width) + update).astype(low).reshape(tokens.shape)
    weighted = grad_normed.astype(jnp.float32) * norm_gain
    first_mean = jnp.mean(weighted, axis=-1, keepdims=True)
    second_mean = jnp.mean(weighted * scaled, axis=-1, keepdims=True)
    grad_rows = inverse * (weighted - first_mean - scaled * second_mean)
    grad_rows = grad_rows + grad_output[0].astype(jnp.float32)
    return (block_rows[None], grad_rows.astype(low)[None], grad_weight)


def solution(mesh):
    fine = Mesh(mesh.devices.reshape(SIZES + (mesh.shape["dp"],)), PARTS + ("dp",))
    rows = P("dp", PARTS, None, None)
    weight = P(PARTS, None)
    return jax.shard_map(
        on_device,
        mesh=fine,
        in_specs=(rows, P("dp", None, None), rows, P(), weight, weight, weight, weight),
        out_specs=(rows, rows, weight),
        check_vma=False,
    )
```

```python
import math

import jax
import jax.numpy as jnp
from jax import lax
from jax.experimental import pallas as pl
from jax.experimental.pallas import tpu as pltpu
from jax.sharding import Mesh
from jax.sharding import PartitionSpec as P

HEADS = 8
NORM_EPS = 1e-06
PARTS = ("x", "y", "core")
SIZES = (4, 8, 2)


def dot(left, right, contract):
    return lax.dot_general(
        left, right, (contract, ((), ())), preferred_element_type=jnp.float32
    )


NN = ((1,), (0,))
NT = ((1,), (1,))
TN = ((0,), (0,))


def cell_kernel(normed_ref, grad_ref, row_ref, col_ref, whole_ref, pick_ref,
                sent_ref, own_ref, other_ref, out_ref, qkv_ref):
    low = jnp.bfloat16
    _, lines, depth, _ = whole_ref.shape
    depth //= 2
    att, width = out_ref.shape
    size = att // HEADS
    half = depth // 2
    scale = 1.0 / math.sqrt(size)
    for d in range(SIZES[0] * SIZES[1] * SIZES[2]):
        x, y, core = d // (lines * 2), d // 2 % lines, d % 2
        piece = whole_ref.at[x * 2 + core, y]
        qkv_ref[d * depth:(d + 1) * depth, :2 * att] = piece[:depth, :]
        qkv_ref[d * depth:(d + 1) * depth, 2 * att:] = piece[depth:, :att]
        out_ref[d * half:(d + 1) * half, :att] = piece[depth:depth + half, att:]
        out_ref[d * half:(d + 1) * half, att:] = piece[depth + half:, att:]
    qkv = dot(normed_ref[...], qkv_ref[...], NN).astype(low)
    grad_mixed = dot(grad_ref[...], out_ref[...], NT).astype(low)
    same = row_ref[...] == col_ref[...]
    mixed, grad_q, grad_k, grad_v = [], [], [], []
    for h in range(HEADS):
        q = qkv[:, h * size:(h + 1) * size]
        k = qkv[:, att + h * size:att + (h + 1) * size]
        v = qkv[:, 2 * att + h * size:2 * att + (h + 1) * size]
        g = grad_mixed[:, h * size:(h + 1) * size]
        scores = jnp.where(same, dot(q, k, NT) * scale, -jnp.inf)
        expons = jnp.exp(scores - jnp.max(scores, axis=-1, keepdims=True))
        probs = expons / jnp.sum(expons, axis=-1, keepdims=True)
        probs_low = probs.astype(low)
        mixed.append(dot(probs_low, v, NN).astype(low))
        grad_probs = dot(g, v, NT)
        centre = jnp.sum(probs * grad_probs, axis=-1, keepdims=True)
        grad_scores = (probs * (grad_probs - centre) * scale).astype(low)
        grad_q.append(dot(grad_scores, k, NN).astype(low))
        grad_k.append(dot(grad_scores, q, TN).astype(low))
        grad_v.append(dot(probs_low, g, TN).astype(low))
    mixed = jnp.concatenate(mixed, axis=1)
    sent_ref[:, :att] = mixed
    own_ref[...] = dot(mixed, pick_ref[0], NN).astype(low)
    other_ref[...] = dot(mixed, pick_ref[1], NN).astype(low)
    grads = jnp.concatenate(grad_q + grad_k + grad_v, axis=1)
    sent_ref[:, att:] = dot(grads, qkv_ref[...], NT).astype(low)


def cell_part(normed, grad, cells, whole, pick, interpret=False):
    rows, width = normed.shape
    att = pick.shape[1]
    low = jnp.bfloat16
    return pl.pallas_call(
        cell_kernel,
        out_shape=(
            jax.ShapeDtypeStruct((rows, att + width), low),
            jax.ShapeDtypeStruct((rows, att // 2), low),
            jax.ShapeDtypeStruct((rows, att // 2), low),
            jax.ShapeDtypeStruct((att, width), low),
        ),
        scratch_shapes=[pltpu.VMEM((width, 3 * att), low)],
        compiler_params=pltpu.CompilerParams(vmem_limit_bytes=56 << 20),
        interpret=interpret,
    )(normed, grad, cells[:, None], cells[None, :], whole, pick)


def weight_kernel(place_ref, own_ref, got_ref, grad_ref, got_grad_ref, *rest):
    outs, total = rest[:-1], rest[-1]
    total[...] = dot(own_ref[...], grad_ref[...], TN) + dot(
        got_ref[...], got_grad_ref[...], TN
    )
    rows = total.shape[0] // len(outs)
    for k, out in enumerate(outs):
        start = pl.multiple_of(rows * lax.rem(place_ref[0] + k, len(outs)), rows)
        out[...] = total[pl.ds(start, rows), :].astype(out.dtype)


def weight_part(place, own, got, grad, got_grad, interpret=False):
    count = SIZES[0]
    rows, width = own.shape[1] // count, grad.shape[1]
    return pl.pallas_call(
        weight_kernel,
        out_shape=tuple(
            jax.ShapeDtypeStruct((rows, width), jnp.bfloat16 if k else jnp.float32)
            for k in range(count)
        ),
        in_specs=[pl.BlockSpec(memory_space=pltpu.SMEM)]
        + [pl.BlockSpec(memory_space=pltpu.VMEM)] * 4,
        scratch_shapes=[pltpu.VMEM((own.shape[1], width), jnp.float32)],
        compiler_params=pltpu.CompilerParams(vmem_limit_bytes=32 << 20),
        interpret=interpret,
    )(place, own, got, grad, got_grad)


def exchange(values, axis):
    return lax.all_to_all(values, axis, split_axis=0, concat_axis=0, tiled=True)


def shift(values, axis, step, size):
    return lax.ppermute(values, axis, [(i, (i + step) % size) for i in range(size)])


def on_device(frame_tokens, visible, grad_output, norm_gain,
              query_weight, key_weight, value_weight, output_weight):
    low = jnp.bfloat16
    clips = lax.axis_size("dp")
    shards = SIZES[0] * SIZES[1] * SIZES[2]
    tokens = frame_tokens[0]
    frames, groups, width = tokens.shape
    depth, att = query_weight.shape
    me = lax.axis_index(PARTS)
    core = lax.axis_index("core")

    folded = jnp.concatenate(
        [output_weight[:, :width // 2], output_weight[:, width // 2:]], axis=0
    )
    share = jnp.concatenate(
        [
            jnp.concatenate([query_weight, key_weight], axis=1),
            jnp.concatenate([value_weight, folded], axis=1),
        ],
        axis=0,
    )
    line = exchange(jnp.broadcast_to(share[None], (SIZES[1],) + share.shape), "y")
    whole = lax.all_gather(line, ("x", "core"), axis=0, tiled=False)

    values = tokens.astype(jnp.float32)
    centered = values - jnp.mean(values, axis=-1, keepdims=True)
    inverse = lax.rsqrt(jnp.mean(centered * centered, axis=-1, keepdims=True) + NORM_EPS)
    scaled = centered * inverse
    normed = (scaled * norm_gain).astype(low)

    def to_cells(rows):
        sent = rows.transpose(1, 0, 2).reshape(shards, 2, -1)
        return exchange(sent, PARTS).reshape(shards * frames, -1)

    normed_cells = to_cells(normed)
    grad_cells = to_cells(grad_output[0])
    grad_got = shift(grad_cells, "core", 1, 2)
    cells = lax.dynamic_slice_in_dim(visible[0], me, 1, 1)[:, 0]

    per = att // shards
    column = jnp.arange(att, dtype=jnp.int32)
    x, y = column // (per * 16), column // (per * 2) % 8
    place = (x * 8 + y) * per + column % per
    side = column // per % 2
    at = place[:, None] == jnp.arange(att // 2, dtype=jnp.int32)[None, :]
    pick = jnp.stack(
        [at & (side == core)[:, None], at & (side != core)[:, None]]
    ).astype(low)

    sent, own, other, whole_out = cell_part(
        normed_cells, grad_cells, cells, whole, pick
    )
    got = shift(other, "core", 1, 2)
    back = exchange(sent.reshape(shards, 2, -1), PARTS)
    rows = back.reshape(shards, frames, att + width).transpose(1, 0, 2)
    mixed, grad_normed = rows[:, :, :att], rows[:, :, att:]

    slabs = weight_part(
        lax.axis_index("x").astype(jnp.int32)[None], own, got, grad_cells, grad_got
    )
    part = slabs[0]
    for k in range(1, SIZES[0]):
        part = part + shift(slabs[k], "x", k, SIZES[0]).astype(jnp.float32)
    part = part.astype(low).reshape(SIZES[1], 2, -1)
    part, _ = lax.optimization_barrier((part, back))
    part = jnp.sum(exchange(part, "y").astype(jnp.float32), axis=0).astype(low)
    part = exchange(jnp.broadcast_to(part[None], (clips,) + part.shape), "dp")
    grad_weight = jnp.sum(part.astype(jnp.float32), axis=0).reshape(per, width)

    flat_mixed = mixed.reshape(-1, att)
    update = jnp.dot(flat_mixed, whole_out, preferred_element_type=jnp.float32)
    block_rows = (values.reshape(-1, width) + update).astype(low).reshape(tokens.shape)
    weighted = grad_normed.astype(jnp.float32) * norm_gain
    first_mean = jnp.mean(weighted, axis=-1, keepdims=True)
    second_mean = jnp.mean(weighted * scaled, axis=-1, keepdims=True)
    grad_rows = inverse * (weighted - first_mean - scaled * second_mean)
    grad_rows = grad_rows + grad_output[0].astype(jnp.float32)
    return (block_rows[None], grad_rows.astype(low)[None], grad_weight)


def solution(mesh):
    fine = Mesh(mesh.devices.reshape(SIZES + (mesh.shape["dp"],)), PARTS + ("dp",))
    rows = P("dp", PARTS, None, None)
    weight = P(PARTS, None)
    return jax.shard_map(
        on_device,
        mesh=fine,
        in_specs=(rows, P("dp", None, None), rows, P(), weight, weight, weight, weight),
        out_specs=(rows, rows, weight),
        check_vma=False,
    )
```

```python
import math

import jax
import jax.numpy as jnp
from jax import lax
from jax.experimental import pallas as pl
from jax.experimental.pallas import tpu as pltpu
from jax.sharding import Mesh
from jax.sharding import PartitionSpec as P

HEADS = 8
NORM_EPS = 1e-06
PARTS = ("x", "y", "core")
SIZES = (4, 8, 2)


def dot(left, right, contract):
    return lax.dot_general(
        left, right, (contract, ((), ())), preferred_element_type=jnp.float32
    )


NN = ((1,), (0,))
NT = ((1,), (1,))
TN = ((0,), (0,))


def cell_kernel(place_ref, normed_ref, grad_ref, row_ref, col_ref, pick_ref, *rest):
    pieces = rest[:10]
    sent_ref, own_ref, other_ref, out_ref, qkv_ref, whole_ref, arrived = rest[10:]
    low = jnp.bfloat16
    _, lines, depth, _ = whole_ref.shape
    depth //= 2
    copies = []
    for i, piece in enumerate(pieces):
        step = (0, 3, 1, 2, 2)[i % 5]
        at = lax.rem(place_ref[0] + step, 4) * 2 + lax.rem(place_ref[1] + i // 5, 2)
        target = whole_ref.at[at]
        if i % 5 > 2:
            target = target.at[pl.ds((i % 5 - 3) * (lines // 2), lines // 2)]
        copies.append(pltpu.make_async_copy(piece, target, arrived.at[i]))
    for copy in copies:
        copy.start()
    for copy in copies:
        copy.wait()
    att, width = out_ref.shape
    size = att // HEADS
    half = depth // 2
    scale = 1.0 / math.sqrt(size)
    for d in range(SIZES[0] * SIZES[1] * SIZES[2]):
        x, y, core = d // (lines * 2), d // 2 % lines, d % 2
        piece = whole_ref.at[x * 2 + core, y]
        qkv_ref[d * depth:(d + 1) * depth, :2 * att] = piece[:depth, :]
        qkv_ref[d * depth:(d + 1) * depth, 2 * att:] = piece[depth:, :att]
        out_ref[d * half:(d + 1) * half, :att] = piece[depth:depth + half, att:]
        out_ref[d * half:(d + 1) * half, att:] = piece[depth + half:, att:]
    qkv = dot(normed_ref[...], qkv_ref[...], NN).astype(low)
    grad_mixed = dot(grad_ref[...], out_ref[...], NT).astype(low)
    same = row_ref[...] == col_ref[...]
    mixed, grad_q, grad_k, grad_v = [], [], [], []
    for h in range(HEADS):
        q = qkv[:, h * size:(h + 1) * size]
        k = qkv[:, att + h * size:att + (h + 1) * size]
        v = qkv[:, 2 * att + h * size:2 * att + (h + 1) * size]
        g = grad_mixed[:, h * size:(h + 1) * size]
        scores = jnp.where(same, dot(q, k, NT) * scale, -jnp.inf)
        expons = jnp.exp(scores - jnp.max(scores, axis=-1, keepdims=True))
        probs = expons / jnp.sum(expons, axis=-1, keepdims=True)
        probs_low = probs.astype(low)
        mixed.append(dot(probs_low, v, NN).astype(low))
        grad_probs = dot(g, v, NT)
        centre = jnp.sum(probs * grad_probs, axis=-1, keepdims=True)
        grad_scores = (probs * (grad_probs - centre) * scale).astype(low)
        grad_q.append(dot(grad_scores, k, NN).astype(low))
        grad_k.append(dot(grad_scores, q, TN).astype(low))
        grad_v.append(dot(probs_low, g, TN).astype(low))
    mixed = jnp.concatenate(mixed, axis=1)
    sent_ref[:, :att] = mixed
    own_ref[...] = dot(mixed, pick_ref[0], NN).astype(low)
    other_ref[...] = dot(mixed, pick_ref[1], NN).astype(low)
    grads = jnp.concatenate(grad_q + grad_k + grad_v, axis=1)
    sent_ref[:, att:] = dot(grads, qkv_ref[...], NT).astype(low)


def cell_part(place, normed, grad, cells, pieces, pick, interpret=False):
    rows, width = normed.shape
    att = pick.shape[1]
    low = jnp.bfloat16
    return pl.pallas_call(
        cell_kernel,
        out_shape=(
            jax.ShapeDtypeStruct((rows, att + width), low),
            jax.ShapeDtypeStruct((rows, att // 2), low),
            jax.ShapeDtypeStruct((rows, att // 2), low),
            jax.ShapeDtypeStruct((att, width), low),
        ),
        in_specs=[pl.BlockSpec(memory_space=pltpu.SMEM)]
        + [pl.BlockSpec(memory_space=pltpu.VMEM)] * 5
        + [pl.BlockSpec(memory_space=pl.ANY)] * len(pieces),
        scratch_shapes=[
            pltpu.VMEM((width, 3 * att), low),
            pltpu.VMEM((SIZES[0] * SIZES[2],) + pieces[0].shape, low),
            pltpu.SemaphoreType.DMA((len(pieces),)),
        ],
        compiler_params=pltpu.CompilerParams(vmem_limit_bytes=56 << 20),
        interpret=interpret,
    )(place, normed, grad, cells[:, None], cells[None, :], pick, *pieces)


def weight_kernel(place_ref, own_ref, got_ref, grad_ref, got_grad_ref, *rest):
    outs, total = rest[:-1], rest[-1]
    total[...] = dot(own_ref[...], grad_ref[...], TN) + dot(
        got_ref[...], got_grad_ref[...], TN
    )
    rows = total.shape[0] // len(outs)
    for k, out in enumerate(outs):
        start = pl.multiple_of(rows * lax.rem(place_ref[0] + k, len(outs)), rows)
        out[...] = total[pl.ds(start, rows), :].astype(out.dtype)


def weight_part(place, own, got, grad, got_grad, interpret=False):
    count = SIZES[0]
    rows, width = own.shape[1] // count, grad.shape[1]
    return pl.pallas_call(
        weight_kernel,
        out_shape=tuple(
            jax.ShapeDtypeStruct((rows, width), jnp.bfloat16 if k else jnp.float32)
            for k in range(count)
        ),
        in_specs=[pl.BlockSpec(memory_space=pltpu.SMEM)]
        + [pl.BlockSpec(memory_space=pltpu.VMEM)] * 4,
        scratch_shapes=[pltpu.VMEM((own.shape[1], width), jnp.float32)],
        compiler_params=pltpu.CompilerParams(vmem_limit_bytes=32 << 20),
        interpret=interpret,
    )(place, own, got, grad, got_grad)


def exchange(values, axis):
    return lax.all_to_all(values, axis, split_axis=0, concat_axis=0, tiled=True)


def shift(values, axis, step, size):
    return lax.ppermute(values, axis, [(i, (i + step) % size) for i in range(size)])


def on_device(frame_tokens, visible, grad_output, norm_gain,
              query_weight, key_weight, value_weight, output_weight):
    low = jnp.bfloat16
    clips = lax.axis_size("dp")
    shards = SIZES[0] * SIZES[1] * SIZES[2]
    tokens = frame_tokens[0]
    frames, groups, width = tokens.shape
    depth, att = query_weight.shape
    me = lax.axis_index(PARTS)
    core = lax.axis_index("core")

    folded = jnp.concatenate(
        [output_weight[:, :width // 2], output_weight[:, width // 2:]], axis=0
    )
    share = jnp.concatenate(
        [
            jnp.concatenate([query_weight, key_weight], axis=1),
            jnp.concatenate([value_weight, folded], axis=1),
        ],
        axis=0,
    )
    line = exchange(jnp.broadcast_to(share[None], (SIZES[1],) + share.shape), "y")
    left, right = shift(line, "x", 1, SIZES[0]), shift(line, "x", -1, SIZES[0])
    half = SIZES[1] // 2
    far = (shift(left[:half], "x", 1, SIZES[0]), shift(right[half:], "x", -1, SIZES[0]))
    pieces = (line, left, right) + far
    pieces += tuple(shift(piece, "core", 1, SIZES[2]) for piece in pieces)

    values = tokens.astype(jnp.float32)
    centered = values - jnp.mean(values, axis=-1, keepdims=True)
    inverse = lax.rsqrt(jnp.mean(centered * centered, axis=-1, keepdims=True) + NORM_EPS)
    scaled = centered * inverse
    normed = (scaled * norm_gain).astype(low)

    def to_cells(rows):
        sent = rows.transpose(1, 0, 2).reshape(shards, 2, -1)
        return exchange(sent, PARTS).reshape(shards * frames, -1)

    normed_cells = to_cells(normed)
    grad_cells = to_cells(grad_output[0])
    grad_got = shift(grad_cells, "core", 1, 2)
    cells = lax.dynamic_slice_in_dim(visible[0], me, 1, 1)[:, 0]

    per = att // shards
    column = jnp.arange(att, dtype=jnp.int32)
    x, y = column // (per * 16), column // (per * 2) % 8
    place = (x * 8 + y) * per + column % per
    side = column // per % 2
    at = place[:, None] == jnp.arange(att // 2, dtype=jnp.int32)[None, :]
    pick = jnp.stack(
        [at & (side == core)[:, None], at & (side != core)[:, None]]
    ).astype(low)

    spot = jnp.stack([lax.axis_index("x"), core]).astype(jnp.int32)
    sent, own, other, whole_out = cell_part(
        spot, normed_cells, grad_cells, cells, pieces, pick
    )
    got = shift(other, "core", 1, 2)
    back = exchange(sent.reshape(shards, 2, -1), PARTS)
    rows = back.reshape(shards, frames, att + width).transpose(1, 0, 2)
    mixed, grad_normed = rows[:, :, :att], rows[:, :, att:]

    slabs = weight_part(
        lax.axis_index("x").astype(jnp.int32)[None], own, got, grad_cells, grad_got
    )
    part = slabs[0]
    for k in range(1, SIZES[0]):
        part = part + shift(slabs[k], "x", k, SIZES[0]).astype(jnp.float32)
    part = part.astype(low).reshape(SIZES[1], 2, -1)
    part, _ = lax.optimization_barrier((part, back))
    part = jnp.sum(exchange(part, "y").astype(jnp.float32), axis=0).astype(low)
    part = exchange(jnp.broadcast_to(part[None], (clips,) + part.shape), "dp")
    grad_weight = jnp.sum(part.astype(jnp.float32), axis=0).reshape(per, width)

    flat_mixed = mixed.reshape(-1, att)
    update = jnp.dot(flat_mixed, whole_out, preferred_element_type=jnp.float32)
    block_rows = (values.reshape(-1, width) + update).astype(low).reshape(tokens.shape)
    weighted = grad_normed.astype(jnp.float32) * norm_gain
    first_mean = jnp.mean(weighted, axis=-1, keepdims=True)
    second_mean = jnp.mean(weighted * scaled, axis=-1, keepdims=True)
    grad_rows = inverse * (weighted - first_mean - scaled * second_mean)
    grad_rows = grad_rows + grad_output[0].astype(jnp.float32)
    return (block_rows[None], grad_rows.astype(low)[None], grad_weight)


def solution(mesh):
    fine = Mesh(mesh.devices.reshape(SIZES + (mesh.shape["dp"],)), PARTS + ("dp",))
    rows = P("dp", PARTS, None, None)
    weight = P(PARTS, None)
    return jax.shard_map(
        on_device,
        mesh=fine,
        in_specs=(rows, P("dp", None, None), rows, P(), weight, weight, weight, weight),
        out_specs=(rows, rows, weight),
        check_vma=False,
    )
```

```python
import math

import jax
import jax.numpy as jnp
from jax import lax
from jax.experimental import pallas as pl
from jax.experimental.pallas import tpu as pltpu
from jax.sharding import Mesh
from jax.sharding import PartitionSpec as P


HEADS = 8
NORM_EPS = 1e-06
PARTS = ("x", "y", "core")
SIZES = (4, 8, 2)


def dot(left, right, contract):
    return lax.dot_general(
        left, right, (contract, ((), ())), preferred_element_type=jnp.float32
    )


NN = ((1,), (0,))
NT = ((1,), (1,))
TN = ((0,), (0,))


def cell_kernel(place_ref, normed_ref, grad_ref, row_ref, col_ref, pick_ref, *rest):
    pieces = rest[:8]
    sent_ref, own_ref, other_ref, out_ref, qkv_ref, whole_ref, arrived = rest[8:]
    low = jnp.bfloat16
    _, lines, depth, _ = whole_ref.shape
    depth //= 2
    copies = []
    for i, piece in enumerate(pieces):
        step = (0, 3, 1, 2)[i % 4]
        at = lax.rem(place_ref[0] + step, 4) * 2 + lax.rem(place_ref[1] + i // 4, 2)
        copies.append(pltpu.make_async_copy(piece, whole_ref.at[at], arrived.at[i]))
    for copy in copies:
        copy.start()
    for copy in copies:
        copy.wait()
    att, _ = out_ref.shape
    size = att // HEADS
    half = depth // 2
    scale = 1.0 / math.sqrt(size)
    for d in range(SIZES[0] * SIZES[1] * SIZES[2]):
        x, y, core = d // (lines * 2), d // 2 % lines, d % 2
        piece = whole_ref.at[x * 2 + core, y]
        qkv_ref[d * depth:(d + 1) * depth, :2 * att] = piece[:depth, :]
        qkv_ref[d * depth:(d + 1) * depth, 2 * att:] = piece[depth:, :att]
        out_ref[d * half:(d + 1) * half, :att] = piece[depth:depth + half, att:]
        out_ref[d * half:(d + 1) * half, att:] = piece[depth + half:, att:]
    qkv = dot(normed_ref[...], qkv_ref[...], NN).astype(low)
    grad_mixed = dot(grad_ref[...], out_ref[...], NT).astype(low)
    same = row_ref[...] == col_ref[...]
    mixed, grad_q, grad_k, grad_v = [], [], [], []
    for h in range(HEADS):
        q = qkv[:, h * size:(h + 1) * size]
        k = qkv[:, att + h * size:att + (h + 1) * size]
        v = qkv[:, 2 * att + h * size:2 * att + (h + 1) * size]
        g = grad_mixed[:, h * size:(h + 1) * size]
        scores = jnp.where(same, dot(q, k, NT) * scale, -jnp.inf)
        expons = jnp.exp(scores - jnp.max(scores, axis=-1, keepdims=True))
        probs = expons / jnp.sum(expons, axis=-1, keepdims=True)
        probs_low = probs.astype(low)
        mixed.append(dot(probs_low, v, NN).astype(low))
        grad_probs = dot(g, v, NT)
        centre = jnp.sum(probs * grad_probs, axis=-1, keepdims=True)
        grad_scores = (probs * (grad_probs - centre) * scale).astype(low)
        grad_q.append(dot(grad_scores, k, NN).astype(low))
        grad_k.append(dot(grad_scores, q, TN).astype(low))
        grad_v.append(dot(probs_low, g, TN).astype(low))
    mixed = jnp.concatenate(mixed, axis=1)
    sent_ref[:, :att] = mixed
    own_ref[...] = dot(mixed, pick_ref[0], NN).astype(low)
    other_ref[...] = dot(mixed, pick_ref[1], NN).astype(low)
    grads = jnp.concatenate(grad_q + grad_k + grad_v, axis=1)
    sent_ref[:, att:] = dot(grads, qkv_ref[...], NT).astype(low)


def cell_part(place, normed, grad, cells, pieces, pick, interpret=False):
    rows, width = normed.shape
    att = pick.shape[1]
    low = jnp.bfloat16
    return pl.pallas_call(
        cell_kernel,
        out_shape=(
            jax.ShapeDtypeStruct((rows, att + width), low),
            jax.ShapeDtypeStruct((rows, att // 2), low),
            jax.ShapeDtypeStruct((rows, att // 2), low),
            jax.ShapeDtypeStruct((att, width), low),
        ),
        in_specs=[pl.BlockSpec(memory_space=pltpu.SMEM)]
        + [pl.BlockSpec(memory_space=pltpu.VMEM)] * 5
        + [pl.BlockSpec(memory_space=pl.ANY)] * len(pieces),
        scratch_shapes=[
            pltpu.VMEM((width, 3 * att), low),
            pltpu.VMEM((SIZES[0] * SIZES[2],) + pieces[0].shape, low),
            pltpu.SemaphoreType.DMA((len(pieces),)),
        ],
        compiler_params=pltpu.CompilerParams(vmem_limit_bytes=56 << 20),
        interpret=interpret,
    )(place, normed, grad, cells[:, None], cells[None, :], pick, *pieces)


def weight_kernel(place_ref, own_ref, got_ref, grad_ref, got_grad_ref, *rest):
    outs, total = rest[:-1], rest[-1]
    total[...] = dot(own_ref[...], grad_ref[...], TN) + dot(
        got_ref[...], got_grad_ref[...], TN
    )
    rows = total.shape[0] // len(outs)
    for k, out in enumerate(outs):
        start = pl.multiple_of(rows * lax.rem(place_ref[0] + k, len(outs)), rows)
        out[...] = total[pl.ds(start, rows), :].astype(out.dtype)


def weight_part(place, own, got, grad, got_grad, interpret=False):
    count = SIZES[0]
    rows, width = own.shape[1] // count, grad.shape[1]
    return pl.pallas_call(
        weight_kernel,
        out_shape=tuple(
            jax.ShapeDtypeStruct((rows, width), jnp.bfloat16 if k else jnp.float32)
            for k in range(count)
        ),
        in_specs=[pl.BlockSpec(memory_space=pltpu.SMEM)]
        + [pl.BlockSpec(memory_space=pltpu.VMEM)] * 4,
        scratch_shapes=[pltpu.VMEM((own.shape[1], width), jnp.float32)],
        compiler_params=pltpu.CompilerParams(vmem_limit_bytes=32 << 20),
        interpret=interpret,
    )(place, own, got, grad, got_grad)


def exchange(values, axis):
    return lax.all_to_all(values, axis, split_axis=0, concat_axis=0, tiled=True)


def shift(values, axis, step, size):
    return lax.ppermute(values, axis, [(i, (i + step) % size) for i in range(size)])


def on_device(frame_tokens, visible, grad_output, norm_gain,
              query_weight, key_weight, value_weight, output_weight):
    low = jnp.bfloat16
    clips = lax.axis_size("dp")
    shards = SIZES[0] * SIZES[1] * SIZES[2]
    tokens = frame_tokens[0]
    frames, _, width = tokens.shape
    _, att = query_weight.shape
    me = lax.axis_index(PARTS)
    core = lax.axis_index("core")

    folded = jnp.concatenate(
        [output_weight[:, :width // 2], output_weight[:, width // 2:]], axis=0
    )
    share = jnp.concatenate(
        [
            jnp.concatenate([query_weight, key_weight], axis=1),
            jnp.concatenate([value_weight, folded], axis=1),
        ],
        axis=0,
    )
    line = exchange(jnp.broadcast_to(share[None], (SIZES[1],) + share.shape), "y")
    left, right = shift(line, "x", 1, SIZES[0]), shift(line, "x", -1, SIZES[0])
    far = shift(right, "x", -1, SIZES[0])
    pieces = (line, left, right, far)
    pieces += tuple(shift(piece, "core", 1, SIZES[2]) for piece in pieces)

    values = tokens.astype(jnp.float32)
    centered = values - jnp.mean(values, axis=-1, keepdims=True)
    inverse = lax.rsqrt(jnp.mean(centered * centered, axis=-1, keepdims=True) + NORM_EPS)
    scaled = centered * inverse
    normed = (scaled * norm_gain).astype(low)

    def to_cells(rows):
        sent = rows.transpose(1, 0, 2).reshape(shards, 2, -1)
        return exchange(sent, PARTS).reshape(shards * frames, -1)

    grad_cells = to_cells(grad_output[0])
    normed_cells = to_cells(normed)
    grad_got = shift(grad_cells, "core", 1, 2)
    cells = lax.dynamic_slice_in_dim(visible[0], me, 1, 1)[:, 0]

    per = att // shards
    column = jnp.arange(att, dtype=jnp.int32)
    x, y = column // (per * 16), column // (per * 2) % 8
    place = (x * 8 + y) * per + column % per
    side = column // per % 2
    at = place[:, None] == jnp.arange(att // 2, dtype=jnp.int32)[None, :]
    pick = jnp.stack(
        [at & (side == core)[:, None], at & (side != core)[:, None]]
    ).astype(low)

    spot = jnp.stack([lax.axis_index("x"), core]).astype(jnp.int32)
    sent, own, other, whole_out = cell_part(
        spot, normed_cells, grad_cells, cells, pieces, pick
    )
    got = shift(other, "core", 1, 2)
    back = exchange(sent.reshape(shards, 2, -1), PARTS)
    rows = back.reshape(shards, frames, att + width).transpose(1, 0, 2)
    mixed, grad_normed = rows[:, :, :att], rows[:, :, att:]

    slabs = weight_part(
        lax.axis_index("x").astype(jnp.int32)[None], own, got, grad_cells, grad_got
    )
    part = slabs[0]
    for k in range(1, SIZES[0]):
        part = part + shift(slabs[k], "x", k, SIZES[0]).astype(jnp.float32)
    part = part.astype(low).reshape(SIZES[1], 2, -1)
    part, _ = lax.optimization_barrier((part, back))
    part = jnp.sum(exchange(part, "y").astype(jnp.float32), axis=0).astype(low)
    part = exchange(jnp.broadcast_to(part[None], (clips,) + part.shape), "dp")
    grad_weight = jnp.sum(part.astype(jnp.float32), axis=0).reshape(per, width)

    flat_mixed = mixed.reshape(-1, att)
    update = jnp.dot(flat_mixed, whole_out, preferred_element_type=jnp.float32)
    block_rows = (values.reshape(-1, width) + update).astype(low).reshape(tokens.shape)
    weighted = grad_normed.astype(jnp.float32) * norm_gain
    first_mean = jnp.mean(weighted, axis=-1, keepdims=True)
    second_mean = jnp.mean(weighted * scaled, axis=-1, keepdims=True)
    grad_rows = inverse * (weighted - first_mean - scaled * second_mean)
    grad_rows = grad_rows + grad_output[0].astype(jnp.float32)
    return (block_rows[None], grad_rows.astype(low)[None], grad_weight)


def solution(mesh):
    fine = Mesh(mesh.devices.reshape(SIZES + (mesh.shape["dp"],)), PARTS + ("dp",))
    rows = P("dp", PARTS, None, None)
    weight = P(PARTS, None)
    return jax.shard_map(
        on_device,
        mesh=fine,
        in_specs=(rows, P("dp", None, None), rows, P(), weight, weight, weight, weight),
        out_specs=(rows, rows, weight),
        check_vma=False,
    )
```

```python
import math

import jax
import jax.numpy as jnp
from jax import lax
from jax.experimental import pallas as pl
from jax.experimental.pallas import tpu as pltpu
from jax.sharding import Mesh
from jax.sharding import PartitionSpec as P


HEADS = 8
NORM_EPS = 1e-06
PARTS = ("x", "y", "core")
SIZES = (4, 8, 2)


def dot(left, right, contract):
    return lax.dot_general(
        left, right, (contract, ((), ())), preferred_element_type=jnp.float32
    )


NN = ((1,), (0,))
NT = ((1,), (1,))
TN = ((0,), (0,))


def cell_kernel(place_ref, normed_ref, grad_ref, row_ref, col_ref, pick_ref, *rest):
    pieces = rest[:8]
    sent_ref, own_ref, other_ref, out_ref, qkv_ref, whole_ref, arrived = rest[8:]
    low = jnp.bfloat16
    _, lines, depth, _ = whole_ref.shape
    depth //= 2
    copies = []
    for i, piece in enumerate(pieces):
        step = (0, 3, 1, 2)[i % 4]
        at = lax.rem(place_ref[0] + step, 4) * 2 + lax.rem(place_ref[1] + i // 4, 2)
        copies.append(pltpu.make_async_copy(piece, whole_ref.at[at], arrived.at[i]))
    for copy in copies:
        copy.start()
    for copy in copies:
        copy.wait()
    att, _ = out_ref.shape
    size = att // HEADS
    half = depth // 2
    scale = 1.0 / math.sqrt(size)
    for d in range(SIZES[0] * SIZES[1] * SIZES[2]):
        x, y, core = d // (lines * 2), d // 2 % lines, d % 2
        piece = whole_ref.at[x * 2 + core, y]
        qkv_ref[d * depth:(d + 1) * depth, :2 * att] = piece[:depth, :]
        qkv_ref[d * depth:(d + 1) * depth, 2 * att:] = piece[depth:, :att]
        out_ref[d * half:(d + 1) * half, :att] = piece[depth:depth + half, att:]
        out_ref[d * half:(d + 1) * half, att:] = piece[depth + half:, att:]
    qkv = dot(normed_ref[...], qkv_ref[...], NN).astype(low)
    grad_mixed = dot(grad_ref[...], out_ref[...], NT).astype(low)
    same = row_ref[...] == col_ref[...]
    mixed, grad_q, grad_k, grad_v = [], [], [], []
    for h in range(HEADS):
        q = qkv[:, h * size:(h + 1) * size]
        k = qkv[:, att + h * size:att + (h + 1) * size]
        v = qkv[:, 2 * att + h * size:2 * att + (h + 1) * size]
        g = grad_mixed[:, h * size:(h + 1) * size]
        scores = jnp.where(same, dot(q, k, NT) * scale, -jnp.inf)
        expons = jnp.exp(scores - jnp.max(scores, axis=-1, keepdims=True))
        probs = expons / jnp.sum(expons, axis=-1, keepdims=True)
        probs_low = probs.astype(low)
        mixed.append(dot(probs_low, v, NN).astype(low))
        grad_probs = dot(g, v, NT)
        centre = jnp.sum(probs * grad_probs, axis=-1, keepdims=True)
        grad_scores = (probs * (grad_probs - centre) * scale).astype(low)
        grad_q.append(dot(grad_scores, k, NN).astype(low))
        grad_k.append(dot(grad_scores, q, TN).astype(low))
        grad_v.append(dot(probs_low, g, TN).astype(low))
    mixed = jnp.concatenate(mixed, axis=1)
    sent_ref[:, :att] = mixed
    own_ref[...] = dot(mixed, pick_ref[0], NN).astype(low)
    other_ref[...] = dot(mixed, pick_ref[1], NN).astype(low)
    grads = jnp.concatenate(grad_q + grad_k + grad_v, axis=1)
    sent_ref[:, att:] = dot(grads, qkv_ref[...], NT).astype(low)


def cell_part(place, normed, grad, cells, pieces, pick, interpret=False):
    rows, width = normed.shape
    att = pick.shape[1]
    low = jnp.bfloat16
    return pl.pallas_call(
        cell_kernel,
        out_shape=(
            jax.ShapeDtypeStruct((rows, att + width), low),
            jax.ShapeDtypeStruct((rows, att // 2), low),
            jax.ShapeDtypeStruct((rows, att // 2), low),
            jax.ShapeDtypeStruct((att, width), low),
        ),
        in_specs=[pl.BlockSpec(memory_space=pltpu.SMEM)]
        + [pl.BlockSpec(memory_space=pltpu.VMEM)] * 5
        + [pl.BlockSpec(memory_space=pl.ANY)] * len(pieces),
        scratch_shapes=[
            pltpu.VMEM((width, 3 * att), low),
            pltpu.VMEM((SIZES[0] * SIZES[2],) + pieces[0].shape, low),
            pltpu.SemaphoreType.DMA((len(pieces),)),
        ],
        compiler_params=pltpu.CompilerParams(vmem_limit_bytes=56 << 20),
        interpret=interpret,
    )(place, normed, grad, cells[:, None], cells[None, :], pick, *pieces)


def weight_kernel(place_ref, own_ref, got_ref, grad_ref, got_grad_ref, *rest):
    outs, total = rest[:-1], rest[-1]
    total[...] = dot(own_ref[...], grad_ref[...], TN) + dot(
        got_ref[...], got_grad_ref[...], TN
    )
    rows = total.shape[0] // len(outs)
    for k, out in enumerate(outs):
        start = pl.multiple_of(rows * lax.rem(place_ref[0] + k, len(outs)), rows)
        out[...] = total[pl.ds(start, rows), :].astype(out.dtype)


def weight_part(place, own, got, grad, got_grad, interpret=False):
    count = SIZES[0]
    rows, width = own.shape[1] // count, grad.shape[1]
    return pl.pallas_call(
        weight_kernel,
        out_shape=tuple(
            jax.ShapeDtypeStruct((rows, width), jnp.bfloat16 if k else jnp.float32)
            for k in range(count)
        ),
        in_specs=[pl.BlockSpec(memory_space=pltpu.SMEM)]
        + [pl.BlockSpec(memory_space=pltpu.VMEM)] * 4,
        scratch_shapes=[pltpu.VMEM((own.shape[1], width), jnp.float32)],
        compiler_params=pltpu.CompilerParams(vmem_limit_bytes=32 << 20),
        interpret=interpret,
    )(place, own, got, grad, got_grad)


def spread_kernel(place_ref, stay_ref, *rest):
    count = SIZES[1]
    came, outs = rest[:-count], rest[-count:]
    total = stay_ref[...]
    for piece in came:
        total = total + piece[...].astype(jnp.float32)
    rows = total.shape[0] // count
    for place in range(count):
        @pl.when(place_ref[0] == place)
        def _():
            for k, out in enumerate(outs):
                start = rows * ((place + k) % count)
                out[...] = total[start:start + rows].astype(out.dtype)


def spread(place, stay, came, interpret=False):
    count = SIZES[1]
    rows, width = stay.shape[0] // count, stay.shape[1]
    return pl.pallas_call(
        spread_kernel,
        out_shape=tuple(
            jax.ShapeDtypeStruct((rows, width), jnp.bfloat16 if k else jnp.float32)
            for k in range(count)
        ),
        in_specs=[pl.BlockSpec(memory_space=pltpu.SMEM)]
        + [pl.BlockSpec(memory_space=pltpu.VMEM)] * (1 + len(came)),
        compiler_params=pltpu.CompilerParams(vmem_limit_bytes=32 << 20),
        interpret=interpret,
    )(place, stay, *came)


def exchange(values, axis):
    return lax.all_to_all(values, axis, split_axis=0, concat_axis=0, tiled=True)


def shift(values, axis, step, size):
    return lax.ppermute(values, axis, [(i, (i + step) % size) for i in range(size)])


def on_device(frame_tokens, visible, grad_output, norm_gain,
              query_weight, key_weight, value_weight, output_weight):
    low = jnp.bfloat16
    clips = lax.axis_size("dp")
    shards = SIZES[0] * SIZES[1] * SIZES[2]
    tokens = frame_tokens[0]
    frames, _, width = tokens.shape
    _, att = query_weight.shape
    me = lax.axis_index(PARTS)
    core = lax.axis_index("core")

    folded = jnp.concatenate(
        [output_weight[:, :width // 2], output_weight[:, width // 2:]], axis=0
    )
    share = jnp.concatenate(
        [
            jnp.concatenate([query_weight, key_weight], axis=1),
            jnp.concatenate([value_weight, folded], axis=1),
        ],
        axis=0,
    )
    line = exchange(jnp.broadcast_to(share[None], (SIZES[1],) + share.shape), "y")
    left, right = shift(line, "x", 1, SIZES[0]), shift(line, "x", -1, SIZES[0])
    far = shift(right, "x", -1, SIZES[0])
    line_other = shift(line, "core", 1, SIZES[2])
    pieces = (line, left, right, far, line_other)
    pieces += tuple(shift(piece, "core", 1, SIZES[2]) for piece in (left, right, far))

    values = tokens.astype(jnp.float32)
    centered = values - jnp.mean(values, axis=-1, keepdims=True)
    inverse = lax.rsqrt(jnp.mean(centered * centered, axis=-1, keepdims=True) + NORM_EPS)
    scaled = centered * inverse
    normed = (scaled * norm_gain).astype(low)

    def to_cells(rows):
        sent = rows.transpose(1, 0, 2).reshape(shards, 2, -1)
        return exchange(sent, PARTS).reshape(shards * frames, -1)

    grad_cells = to_cells(grad_output[0])
    normed_cells = to_cells(normed)
    grad_got = shift(grad_cells, "core", 1, 2)
    cells = lax.dynamic_slice_in_dim(visible[0], me, 1, 1)[:, 0]

    per = att // shards
    column = jnp.arange(att, dtype=jnp.int32)
    x, y = column // (per * 16), column // (per * 2) % 8
    place = (x * 8 + y) * per + column % per
    side = column // per % 2
    at = place[:, None] == jnp.arange(att // 2, dtype=jnp.int32)[None, :]
    pick = jnp.stack(
        [at & (side == core)[:, None], at & (side != core)[:, None]]
    ).astype(low)

    spot = jnp.stack([lax.axis_index("x"), core]).astype(jnp.int32)
    sent, own, other, whole_out = cell_part(
        spot, normed_cells, grad_cells, cells, pieces, pick
    )
    got = shift(other, "core", 1, 2)
    back = exchange(sent.reshape(shards, 2, -1), PARTS)
    rows = back.reshape(shards, frames, att + width).transpose(1, 0, 2)
    mixed, grad_normed = rows[:, :, :att], rows[:, :, att:]

    slabs = weight_part(
        lax.axis_index("x").astype(jnp.int32)[None], own, got, grad_cells, grad_got
    )
    came = [shift(slabs[k], "x", k, SIZES[0]) for k in range(1, SIZES[0])]
    slabs = spread(lax.axis_index("y").astype(jnp.int32)[None], slabs[0], came)
    part = slabs[0]
    for k in range(1, SIZES[1]):
        part = part + shift(slabs[k], "y", k, SIZES[1]).astype(jnp.float32)
    part, _ = lax.optimization_barrier((part.astype(low).reshape(2, -1), back))
    part = exchange(jnp.broadcast_to(part[None], (clips,) + part.shape), "dp")
    grad_weight = jnp.sum(part.astype(jnp.float32), axis=0).reshape(per, width)

    flat_mixed = mixed.reshape(-1, att)
    update = jnp.dot(flat_mixed, whole_out, preferred_element_type=jnp.float32)
    block_rows = (values.reshape(-1, width) + update).astype(low).reshape(tokens.shape)
    weighted = grad_normed.astype(jnp.float32) * norm_gain
    first_mean = jnp.mean(weighted, axis=-1, keepdims=True)
    second_mean = jnp.mean(weighted * scaled, axis=-1, keepdims=True)
    grad_rows = inverse * (weighted - first_mean - scaled * second_mean)
    grad_rows = grad_rows + grad_output[0].astype(jnp.float32)
    return (block_rows[None], grad_rows.astype(low)[None], grad_weight)


def solution(mesh):
    fine = Mesh(mesh.devices.reshape(SIZES + (mesh.shape["dp"],)), PARTS + ("dp",))
    rows = P("dp", PARTS, None, None)
    weight = P(PARTS, None)
    return jax.shard_map(
        on_device,
        mesh=fine,
        in_specs=(rows, P("dp", None, None), rows, P(), weight, weight, weight, weight),
        out_specs=(rows, rows, weight),
        check_vma=False,
    )
```

```python
import math

import jax
import jax.numpy as jnp
from jax import lax
from jax.experimental import pallas as pl
from jax.experimental.pallas import tpu as pltpu
from jax.sharding import Mesh
from jax.sharding import PartitionSpec as P


HEADS = 8
NORM_EPS = 1e-06
PARTS = ("x", "y", "core")
SIZES = (4, 8, 2)


def dot(left, right, contract):
    return lax.dot_general(
        left, right, (contract, ((), ())), preferred_element_type=jnp.float32
    )


NN = ((1,), (0,))
NT = ((1,), (1,))
TN = ((0,), (0,))


def cell_kernel(place_ref, normed_ref, grad_ref, row_ref, col_ref, pick_ref, *rest):
    pieces = rest[:8]
    sent_ref, own_ref, other_ref, out_ref, qkv_ref, whole_ref, arrived = rest[8:]
    low = jnp.bfloat16
    _, lines, depth, _ = whole_ref.shape
    depth //= 2
    copies = []
    for i, piece in enumerate(pieces):
        step = (0, 3, 1, 2)[i % 4]
        at = lax.rem(place_ref[0] + step, 4) * 2 + lax.rem(place_ref[1] + i // 4, 2)
        copies.append(pltpu.make_async_copy(piece, whole_ref.at[at], arrived.at[i]))
    for copy in copies:
        copy.start()
    for copy in copies:
        copy.wait()
    att, _ = out_ref.shape
    size = att // HEADS
    half = depth // 2
    scale = 1.0 / math.sqrt(size)
    for d in range(SIZES[0] * SIZES[1] * SIZES[2]):
        x, y, core = d // (lines * 2), d // 2 % lines, d % 2
        piece = whole_ref.at[x * 2 + core, y]
        qkv_ref[d * depth:(d + 1) * depth, :2 * att] = piece[:depth, :]
        qkv_ref[d * depth:(d + 1) * depth, 2 * att:] = piece[depth:, :att]
        out_ref[d * half:(d + 1) * half, :att] = piece[depth:depth + half, att:]
        out_ref[d * half:(d + 1) * half, att:] = piece[depth + half:, att:]
    qkv = dot(normed_ref[...], qkv_ref[...], NN).astype(low)
    grad_mixed = dot(grad_ref[...], out_ref[...], NT).astype(low)
    same = row_ref[...] == col_ref[...]
    mixed, grad_q, grad_k, grad_v = [], [], [], []
    for h in range(HEADS):
        q = qkv[:, h * size:(h + 1) * size]
        k = qkv[:, att + h * size:att + (h + 1) * size]
        v = qkv[:, 2 * att + h * size:2 * att + (h + 1) * size]
        g = grad_mixed[:, h * size:(h + 1) * size]
        scores = jnp.where(same, dot(q, k, NT) * scale, -jnp.inf)
        expons = jnp.exp(scores - jnp.max(scores, axis=-1, keepdims=True))
        probs = expons / jnp.sum(expons, axis=-1, keepdims=True)
        probs_low = probs.astype(low)
        mixed.append(dot(probs_low, v, NN).astype(low))
        grad_probs = dot(g, v, NT)
        centre = jnp.sum(probs * grad_probs, axis=-1, keepdims=True)
        grad_scores = (probs * (grad_probs - centre) * scale).astype(low)
        grad_q.append(dot(grad_scores, k, NN).astype(low))
        grad_k.append(dot(grad_scores, q, TN).astype(low))
        grad_v.append(dot(probs_low, g, TN).astype(low))
    mixed = jnp.concatenate(mixed, axis=1)
    sent_ref[:, :att] = mixed
    own_ref[...] = dot(mixed, pick_ref[0], NN).astype(low)
    other_ref[...] = dot(mixed, pick_ref[1], NN).astype(low)
    grads = jnp.concatenate(grad_q + grad_k + grad_v, axis=1)
    sent_ref[:, att:] = dot(grads, qkv_ref[...], NT).astype(low)


def cell_part(place, normed, grad, cells, pieces, pick, interpret=False):
    rows, width = normed.shape
    att = pick.shape[1]
    low = jnp.bfloat16
    return pl.pallas_call(
        cell_kernel,
        out_shape=(
            jax.ShapeDtypeStruct((rows, att + width), low),
            jax.ShapeDtypeStruct((rows, att // 2), low),
            jax.ShapeDtypeStruct((rows, att // 2), low),
            jax.ShapeDtypeStruct((att, width), low),
        ),
        in_specs=[pl.BlockSpec(memory_space=pltpu.SMEM)]
        + [pl.BlockSpec(memory_space=pltpu.VMEM)] * 5
        + [pl.BlockSpec(memory_space=pl.ANY)] * len(pieces),
        scratch_shapes=[
            pltpu.VMEM((width, 3 * att), low),
            pltpu.VMEM((SIZES[0] * SIZES[2],) + pieces[0].shape, low),
            pltpu.SemaphoreType.DMA((len(pieces),)),
        ],
        compiler_params=pltpu.CompilerParams(vmem_limit_bytes=56 << 20),
        interpret=interpret,
    )(place, normed, grad, cells[:, None], cells[None, :], pick, *pieces)


def weight_kernel(place_ref, own_ref, got_ref, grad_ref, got_grad_ref, *rest):
    outs, total = rest[:-1], rest[-1]
    total[...] = dot(own_ref[...], grad_ref[...], TN) + dot(
        got_ref[...], got_grad_ref[...], TN
    )
    rows = total.shape[0] // len(outs)
    for k, out in enumerate(outs):
        start = pl.multiple_of(rows * lax.rem(place_ref[0] + k, len(outs)), rows)
        out[...] = total[pl.ds(start, rows), :].astype(out.dtype)


def weight_part(place, own, got, grad, got_grad, interpret=False):
    count = SIZES[0]
    rows, width = own.shape[1] // count, grad.shape[1]
    return pl.pallas_call(
        weight_kernel,
        out_shape=tuple(
            jax.ShapeDtypeStruct((rows, width), jnp.bfloat16 if k else jnp.float32)
            for k in range(count)
        ),
        in_specs=[pl.BlockSpec(memory_space=pltpu.SMEM)]
        + [pl.BlockSpec(memory_space=pltpu.VMEM)] * 4,
        scratch_shapes=[pltpu.VMEM((own.shape[1], width), jnp.float32)],
        compiler_params=pltpu.CompilerParams(vmem_limit_bytes=32 << 20),
        interpret=interpret,
    )(place, own, got, grad, got_grad)


def halve_kernel(bit_ref, stayed_ref, *rest):
    came, stay_ref, send_ref = rest[:-2], rest[-2], rest[-1]
    total = stayed_ref[...]
    for piece in came:
        total = total + piece[...].astype(jnp.float32)
    rows = stay_ref.shape[0]
    for side in range(2):
        @pl.when(bit_ref[0] == side)
        def _():
            stay_ref[...] = total[side * rows:(side + 1) * rows]
            send_ref[...] = total[(1 - side) * rows:(2 - side) * rows].astype(send_ref.dtype)


def halve(bit, stayed, came, interpret=False):
    rows, width = stayed.shape[0] // 2, stayed.shape[1]
    return pl.pallas_call(
        halve_kernel,
        out_shape=(
            jax.ShapeDtypeStruct((rows, width), jnp.float32),
            jax.ShapeDtypeStruct((rows, width), jnp.bfloat16),
        ),
        in_specs=[pl.BlockSpec(memory_space=pltpu.SMEM)]
        + [pl.BlockSpec(memory_space=pltpu.VMEM)] * (1 + len(came)),
        compiler_params=pltpu.CompilerParams(vmem_limit_bytes=32 << 20),
        interpret=interpret,
    )(bit, stayed, *came)


def exchange(values, axis):
    return lax.all_to_all(values, axis, split_axis=0, concat_axis=0, tiled=True)


def shift(values, axis, step, size):
    return lax.ppermute(values, axis, [(i, (i + step) % size) for i in range(size)])


def on_device(frame_tokens, visible, grad_output, norm_gain,
              query_weight, key_weight, value_weight, output_weight):
    low = jnp.bfloat16
    clips = lax.axis_size("dp")
    shards = SIZES[0] * SIZES[1] * SIZES[2]
    tokens = frame_tokens[0]
    frames, _, width = tokens.shape
    _, att = query_weight.shape
    me = lax.axis_index(PARTS)
    core = lax.axis_index("core")

    folded = jnp.concatenate(
        [output_weight[:, :width // 2], output_weight[:, width // 2:]], axis=0
    )
    share = jnp.concatenate(
        [
            jnp.concatenate([query_weight, key_weight], axis=1),
            jnp.concatenate([value_weight, folded], axis=1),
        ],
        axis=0,
    )
    line = exchange(jnp.broadcast_to(share[None], (SIZES[1],) + share.shape), "y")
    left, right = shift(line, "x", 1, SIZES[0]), shift(line, "x", -1, SIZES[0])
    far = shift(right, "x", -1, SIZES[0])
    pieces = (line, left, right, far)
    pieces += tuple(shift(piece, "core", 1, SIZES[2]) for piece in pieces)

    values = tokens.astype(jnp.float32)
    centered = values - jnp.mean(values, axis=-1, keepdims=True)
    inverse = lax.rsqrt(jnp.mean(centered * centered, axis=-1, keepdims=True) + NORM_EPS)
    scaled = centered * inverse
    normed = (scaled * norm_gain).astype(low)

    def to_cells(rows):
        sent = rows.transpose(1, 0, 2).reshape(shards, 2, -1)
        return exchange(sent, PARTS).reshape(shards * frames, -1)

    grad_cells = to_cells(grad_output[0])
    normed_cells = to_cells(normed)
    grad_got = shift(grad_cells, "core", 1, 2)
    cells = lax.dynamic_slice_in_dim(visible[0], me, 1, 1)[:, 0]

    per = att // shards
    column = jnp.arange(att, dtype=jnp.int32)
    x, y = column // (per * 16), column // (per * 2) % 8
    y = y % 2 * 4 + y // 2 % 2 * 2 + y // 4
    place = (x * 8 + y) * per + column % per
    side = column // per % 2
    at = place[:, None] == jnp.arange(att // 2, dtype=jnp.int32)[None, :]
    pick = jnp.stack(
        [at & (side == core)[:, None], at & (side != core)[:, None]]
    ).astype(low)

    spot = jnp.stack([lax.axis_index("x"), core]).astype(jnp.int32)
    sent, own, other, whole_out = cell_part(
        spot, normed_cells, grad_cells, cells, pieces, pick
    )
    got = shift(other, "core", 1, 2)
    back = exchange(sent.reshape(shards, 2, -1), PARTS)
    rows = back.reshape(shards, frames, att + width).transpose(1, 0, 2)
    mixed, grad_normed = rows[:, :, :att], rows[:, :, att:]

    slabs = weight_part(
        lax.axis_index("x").astype(jnp.int32)[None], own, got, grad_cells, grad_got
    )
    came = [shift(slabs[k], "x", k, SIZES[0]) for k in range(1, SIZES[0])]
    stay = slabs[0]
    for level in range(3):
        bit = ((lax.axis_index("y") >> level) & 1).astype(jnp.int32)[None]
        stay, send = halve(bit, stay, came)
        flips = [(i, i ^ (1 << level)) for i in range(SIZES[1])]
        came = [lax.ppermute(send, "y", flips)]
    part = stay + came[0].astype(jnp.float32)
    part, _ = lax.optimization_barrier((part.astype(low).reshape(2, -1), back))
    part = exchange(jnp.broadcast_to(part[None], (clips,) + part.shape), "dp")
    grad_weight = jnp.sum(part.astype(jnp.float32), axis=0).reshape(per, width)

    flat_mixed = mixed.reshape(-1, att)
    update = jnp.dot(flat_mixed, whole_out, preferred_element_type=jnp.float32)
    block_rows = (values.reshape(-1, width) + update).astype(low).reshape(tokens.shape)
    weighted = grad_normed.astype(jnp.float32) * norm_gain
    first_mean = jnp.mean(weighted, axis=-1, keepdims=True)
    second_mean = jnp.mean(weighted * scaled, axis=-1, keepdims=True)
    grad_rows = inverse * (weighted - first_mean - scaled * second_mean)
    grad_rows = grad_rows + grad_output[0].astype(jnp.float32)
    return (block_rows[None], grad_rows.astype(low)[None], grad_weight)


def solution(mesh):
    fine = Mesh(mesh.devices.reshape(SIZES + (mesh.shape["dp"],)), PARTS + ("dp",))
    rows = P("dp", PARTS, None, None)
    weight = P(PARTS, None)
    return jax.shard_map(
        on_device,
        mesh=fine,
        in_specs=(rows, P("dp", None, None), rows, P(), weight, weight, weight, weight),
        out_specs=(rows, rows, weight),
        check_vma=False,
    )
```

```python
import math

import jax
import jax.numpy as jnp
from jax import lax
from jax.experimental import pallas as pl
from jax.experimental.pallas import tpu as pltpu
from jax.sharding import Mesh
from jax.sharding import PartitionSpec as P


HEADS = 8
NORM_EPS = 1e-06
PARTS = ("x", "y", "core")
SIZES = (4, 8, 2)


def dot(left, right, contract):
    return lax.dot_general(
        left, right, (contract, ((), ())), preferred_element_type=jnp.float32
    )


NN = ((1,), (0,))
NT = ((1,), (1,))
TN = ((0,), (0,))


def cell_kernel(place_ref, normed_ref, grad_ref, row_ref, col_ref, pick_ref, *rest):
    pieces = rest[:8]
    sent_ref, own_ref, other_ref, out_ref, qkv_ref, whole_ref, arrived = rest[8:]
    low = jnp.bfloat16
    _, lines, depth, _ = whole_ref.shape
    depth //= 2
    for i, piece in enumerate(pieces):
        step = (0, 3, 1, 2)[i % 4]
        at = lax.rem(place_ref[0] + step, 4) * 2 + lax.rem(place_ref[1] + i // 4, 2)
        pltpu.make_async_copy(piece, whole_ref.at[at], arrived.at[at]).start()
    half = depth // 2
    att, _ = out_ref.shape
    size = att // HEADS
    scale = 1.0 / math.sqrt(size)
    for slot in range(SIZES[0] * SIZES[2]):
        pltpu.make_async_copy(pieces[0], whole_ref.at[slot], arrived.at[slot]).wait()
        for y in range(lines):
            d = (slot // 2 * lines + y) * 2 + slot % 2
            piece = whole_ref.at[slot, y]
            qkv_ref[d * depth:(d + 1) * depth, :2 * att] = piece[:depth, :]
            qkv_ref[d * depth:(d + 1) * depth, 2 * att:] = piece[depth:, :att]
            out_ref[d * half:(d + 1) * half, :att] = piece[depth:depth + half, att:]
            out_ref[d * half:(d + 1) * half, att:] = piece[depth + half:, att:]
    qkv = dot(normed_ref[...], qkv_ref[...], NN).astype(low)
    grad_mixed = dot(grad_ref[...], out_ref[...], NT).astype(low)
    same = row_ref[...] == col_ref[...]
    mixed, grad_q, grad_k, grad_v = [], [], [], []
    for h in range(HEADS):
        q = qkv[:, h * size:(h + 1) * size]
        k = qkv[:, att + h * size:att + (h + 1) * size]
        v = qkv[:, 2 * att + h * size:2 * att + (h + 1) * size]
        g = grad_mixed[:, h * size:(h + 1) * size]
        scores = jnp.where(same, dot(q, k, NT) * scale, -jnp.inf)
        expons = jnp.exp(scores - jnp.max(scores, axis=-1, keepdims=True))
        probs = expons / jnp.sum(expons, axis=-1, keepdims=True)
        probs_low = probs.astype(low)
        mixed.append(dot(probs_low, v, NN).astype(low))
        grad_probs = dot(g, v, NT)
        centre = jnp.sum(probs * grad_probs, axis=-1, keepdims=True)
        grad_scores = (probs * (grad_probs - centre) * scale).astype(low)
        grad_q.append(dot(grad_scores, k, NN).astype(low))
        grad_k.append(dot(grad_scores, q, TN).astype(low))
        grad_v.append(dot(probs_low, g, TN).astype(low))
    mixed = jnp.concatenate(mixed, axis=1)
    sent_ref[:, :att] = mixed
    own_ref[...] = dot(mixed, pick_ref[0], NN).astype(low)
    other_ref[...] = dot(mixed, pick_ref[1], NN).astype(low)
    grads = jnp.concatenate(grad_q + grad_k + grad_v, axis=1)
    sent_ref[:, att:] = dot(grads, qkv_ref[...], NT).astype(low)


def cell_part(place, normed, grad, cells, pieces, pick, interpret=False):
    rows, width = normed.shape
    att = pick.shape[1]
    low = jnp.bfloat16
    return pl.pallas_call(
        cell_kernel,
        out_shape=(
            jax.ShapeDtypeStruct((rows, att + width), low),
            jax.ShapeDtypeStruct((rows, att // 2), low),
            jax.ShapeDtypeStruct((rows, att // 2), low),
            jax.ShapeDtypeStruct((att, width), low),
        ),
        in_specs=[pl.BlockSpec(memory_space=pltpu.SMEM)]
        + [pl.BlockSpec(memory_space=pltpu.VMEM)] * 5
        + [pl.BlockSpec(memory_space=pl.ANY)] * len(pieces),
        scratch_shapes=[
            pltpu.VMEM((width, 3 * att), low),
            pltpu.VMEM((SIZES[0] * SIZES[2],) + pieces[0].shape, low),
            pltpu.SemaphoreType.DMA((len(pieces),)),
        ],
        compiler_params=pltpu.CompilerParams(vmem_limit_bytes=56 << 20),
        interpret=interpret,
    )(place, normed, grad, cells[:, None], cells[None, :], pick, *pieces)


def weight_kernel(place_ref, own_ref, got_ref, grad_ref, got_grad_ref, *rest):
    outs, total = rest[:-1], rest[-1]
    total[...] = dot(own_ref[...], grad_ref[...], TN) + dot(
        got_ref[...], got_grad_ref[...], TN
    )
    rows = total.shape[0] // len(outs)
    for k, out in enumerate(outs):
        start = pl.multiple_of(rows * lax.rem(place_ref[0] + k, len(outs)), rows)
        out[...] = total[pl.ds(start, rows), :].astype(out.dtype)


def weight_part(place, own, got, grad, got_grad, interpret=False):
    count = SIZES[0]
    rows, width = own.shape[1] // count, grad.shape[1]
    return pl.pallas_call(
        weight_kernel,
        out_shape=tuple(
            jax.ShapeDtypeStruct((rows, width), jnp.bfloat16 if k else jnp.float32)
            for k in range(count)
        ),
        in_specs=[pl.BlockSpec(memory_space=pltpu.SMEM)]
        + [pl.BlockSpec(memory_space=pltpu.VMEM)] * 4,
        scratch_shapes=[pltpu.VMEM((own.shape[1], width), jnp.float32)],
        compiler_params=pltpu.CompilerParams(vmem_limit_bytes=32 << 20),
        interpret=interpret,
    )(place, own, got, grad, got_grad)


def exchange(values, axis):
    return lax.all_to_all(values, axis, split_axis=0, concat_axis=0, tiled=True)


def shift(values, axis, step, size):
    return lax.ppermute(values, axis, [(i, (i + step) % size) for i in range(size)])


def on_device(frame_tokens, visible, grad_output, norm_gain,
              query_weight, key_weight, value_weight, output_weight):
    low = jnp.bfloat16
    clips = lax.axis_size("dp")
    shards = SIZES[0] * SIZES[1] * SIZES[2]
    tokens = frame_tokens[0]
    frames, _, width = tokens.shape
    _, att = query_weight.shape
    me = lax.axis_index(PARTS)
    core = lax.axis_index("core")

    folded = jnp.concatenate(
        [output_weight[:, :width // 2], output_weight[:, width // 2:]], axis=0
    )
    share = jnp.concatenate(
        [
            jnp.concatenate([query_weight, key_weight], axis=1),
            jnp.concatenate([value_weight, folded], axis=1),
        ],
        axis=0,
    )
    line = exchange(jnp.broadcast_to(share[None], (SIZES[1],) + share.shape), "y")
    left, right = shift(line, "x", 1, SIZES[0]), shift(line, "x", -1, SIZES[0])
    far = shift(right, "x", -1, SIZES[0])
    pieces = (line, left, right, far)
    pieces += tuple(shift(piece, "core", 1, SIZES[2]) for piece in pieces)

    values = tokens.astype(jnp.float32)
    centered = values - jnp.mean(values, axis=-1, keepdims=True)
    inverse = lax.rsqrt(jnp.mean(centered * centered, axis=-1, keepdims=True) + NORM_EPS)
    scaled = centered * inverse
    normed = (scaled * norm_gain).astype(low)

    def to_cells(rows):
        sent = rows.transpose(1, 0, 2).reshape(shards, 2, -1)
        return exchange(sent, PARTS).reshape(shards * frames, -1)

    grad_cells = to_cells(grad_output[0])
    normed_cells = to_cells(normed)
    grad_got = shift(grad_cells, "core", 1, 2)
    cells = lax.dynamic_slice_in_dim(visible[0], me, 1, 1)[:, 0]

    per = att // shards
    column = jnp.arange(att, dtype=jnp.int32)
    x, y = column // (per * 16), column // (per * 2) % 8
    place = (x * 8 + y) * per + column % per
    side = column // per % 2
    at = place[:, None] == jnp.arange(att // 2, dtype=jnp.int32)[None, :]
    pick = jnp.stack(
        [at & (side == core)[:, None], at & (side != core)[:, None]]
    ).astype(low)

    spot = jnp.stack([lax.axis_index("x"), core]).astype(jnp.int32)
    sent, own, other, whole_out = cell_part(
        spot, normed_cells, grad_cells, cells, pieces, pick
    )
    got = shift(other, "core", 1, 2)
    back = exchange(sent.reshape(shards, 2, -1), PARTS)
    rows = back.reshape(shards, frames, att + width).transpose(1, 0, 2)
    mixed, grad_normed = rows[:, :, :att], rows[:, :, att:]

    slabs = weight_part(
        lax.axis_index("x").astype(jnp.int32)[None], own, got, grad_cells, grad_got
    )
    part = slabs[0]
    for k in range(1, SIZES[0]):
        part = part + shift(slabs[k], "x", k, SIZES[0]).astype(jnp.float32)
    part = part.astype(low).reshape(SIZES[1], 2, -1)
    part, _ = lax.optimization_barrier((part, back))
    part = jnp.sum(exchange(part, "y").astype(jnp.float32), axis=0).astype(low)
    part = exchange(jnp.broadcast_to(part[None], (clips,) + part.shape), "dp")
    grad_weight = jnp.sum(part.astype(jnp.float32), axis=0).reshape(per, width)

    flat_mixed = mixed.reshape(-1, att)
    update = jnp.dot(flat_mixed, whole_out, preferred_element_type=jnp.float32)
    block_rows = (values.reshape(-1, width) + update).astype(low).reshape(tokens.shape)
    weighted = grad_normed.astype(jnp.float32) * norm_gain
    first_mean = jnp.mean(weighted, axis=-1, keepdims=True)
    second_mean = jnp.mean(weighted * scaled, axis=-1, keepdims=True)
    grad_rows = inverse * (weighted - first_mean - scaled * second_mean)
    grad_rows = grad_rows + grad_output[0].astype(jnp.float32)
    return (block_rows[None], grad_rows.astype(low)[None], grad_weight)


def solution(mesh):
    fine = Mesh(mesh.devices.reshape(SIZES + (mesh.shape["dp"],)), PARTS + ("dp",))
    rows = P("dp", PARTS, None, None)
    weight = P(PARTS, None)
    return jax.shard_map(
        on_device,
        mesh=fine,
        in_specs=(rows, P("dp", None, None), rows, P(), weight, weight, weight, weight),
        out_specs=(rows, rows, weight),
        check_vma=False,
    )
```

```python
import math

import jax
import jax.numpy as jnp
from jax import lax
from jax.experimental import pallas as pl
from jax.experimental.pallas import tpu as pltpu
from jax.sharding import Mesh
from jax.sharding import PartitionSpec as P


HEADS = 8
NORM_EPS = 1e-06
PARTS = ("x", "y", "core")
SIZES = (4, 8, 2)


def dot(left, right, contract):
    return lax.dot_general(
        left, right, (contract, ((), ())), preferred_element_type=jnp.float32
    )


NN = ((1,), (0,))
NT = ((1,), (1,))
TN = ((0,), (0,))


def cell_kernel(place_ref, normed_ref, grad_ref, row_ref, col_ref, pick_ref, *rest):
    pieces = rest[:8]
    sent_ref, own_ref, other_ref, out_ref, qkv_ref, whole_ref, arrived = rest[8:]
    low = jnp.bfloat16
    _, lines, depth, _ = whole_ref.shape
    depth //= 2
    copies = []
    for i, piece in enumerate(pieces):
        step = (0, 3, 1, 2)[i % 4]
        at = lax.rem(place_ref[0] + step, 4) * 2 + lax.rem(place_ref[1] + i // 4, 2)
        copies.append(pltpu.make_async_copy(piece, whole_ref.at[at], arrived.at[i]))
    for copy in copies:
        copy.start()
    for copy in copies:
        copy.wait()
    att, _ = out_ref.shape
    size = att // HEADS
    half = depth // 2
    scale = 1.0 / math.sqrt(size)
    for d in range(SIZES[0] * SIZES[1] * SIZES[2]):
        x, y, core = d // (lines * 2), d // 2 % lines, d % 2
        piece = whole_ref.at[x * 2 + core, y]
        qkv_ref[d * depth:(d + 1) * depth, :2 * att] = piece[:depth, :]
        qkv_ref[d * depth:(d + 1) * depth, 2 * att:] = piece[depth:, :att]
        out_ref[d * half:(d + 1) * half, :att] = piece[depth:depth + half, att:]
        out_ref[d * half:(d + 1) * half, att:] = piece[depth + half:, att:]
    qkv = dot(normed_ref[...], qkv_ref[...], NN).astype(low)
    grad_mixed = dot(grad_ref[...], out_ref[...], NT).astype(low)
    same = row_ref[...] == col_ref[...]
    mixed, grad_q, grad_k, grad_v = [], [], [], []
    for first in range(0, HEADS, 4):
        heads = range(first, first + 4)
        q = [qkv[:, h * size:(h + 1) * size] for h in heads]
        k = [qkv[:, att + h * size:att + (h + 1) * size] for h in heads]
        v = [qkv[:, 2 * att + h * size:2 * att + (h + 1) * size] for h in heads]
        g = [grad_mixed[:, h * size:(h + 1) * size] for h in heads]
        scores = [dot(a, b, NT) for a, b in zip(q, k)]
        grad_probs = [dot(a, b, NT) for a, b in zip(g, v)]
        scores = [jnp.where(same, a * scale, -jnp.inf) for a in scores]
        tops = [jnp.max(a, axis=-1, keepdims=True) for a in scores]
        expons = [jnp.exp(a - b) for a, b in zip(scores, tops)]
        sums = [jnp.sum(a, axis=-1, keepdims=True) for a in expons]
        probs = [a * pl.reciprocal(b) for a, b in zip(expons, sums)]
        probs_low = [a.astype(low) for a in probs]
        mixed += [dot(a, b, NN).astype(low) for a, b in zip(probs_low, v)]
        grad_v += [dot(a, b, TN).astype(low) for a, b in zip(probs_low, g)]
        centres = [
            jnp.sum(a * b, axis=-1, keepdims=True) for a, b in zip(probs, grad_probs)
        ]
        grad_scores = [
            (a * (b - c) * scale).astype(low)
            for a, b, c in zip(probs, grad_probs, centres)
        ]
        grad_q += [dot(a, b, NN).astype(low) for a, b in zip(grad_scores, k)]
        grad_k += [dot(a, b, TN).astype(low) for a, b in zip(grad_scores, q)]
    mixed = jnp.concatenate(mixed, axis=1)
    sent_ref[:, :att] = mixed
    own_ref[...] = dot(mixed, pick_ref[0], NN).astype(low)
    other_ref[...] = dot(mixed, pick_ref[1], NN).astype(low)
    grads = jnp.concatenate(grad_q + grad_k + grad_v, axis=1)
    sent_ref[:, att:] = dot(grads, qkv_ref[...], NT).astype(low)


def cell_part(place, normed, grad, cells, pieces, pick, interpret=False):
    rows, width = normed.shape
    att = pick.shape[1]
    low = jnp.bfloat16
    return pl.pallas_call(
        cell_kernel,
        out_shape=(
            jax.ShapeDtypeStruct((rows, att + width), low),
            jax.ShapeDtypeStruct((rows, att // 2), low),
            jax.ShapeDtypeStruct((rows, att // 2), low),
            jax.ShapeDtypeStruct((att, width), low),
        ),
        in_specs=[pl.BlockSpec(memory_space=pltpu.SMEM)]
        + [pl.BlockSpec(memory_space=pltpu.VMEM)] * 5
        + [pl.BlockSpec(memory_space=pl.ANY)] * len(pieces),
        scratch_shapes=[
            pltpu.VMEM((width, 3 * att), low),
            pltpu.VMEM((SIZES[0] * SIZES[2],) + pieces[0].shape, low),
            pltpu.SemaphoreType.DMA((len(pieces),)),
        ],
        compiler_params=pltpu.CompilerParams(vmem_limit_bytes=56 << 20),
        interpret=interpret,
    )(place, normed, grad, cells[:, None], cells[None, :], pick, *pieces)


def weight_kernel(place_ref, own_ref, got_ref, grad_ref, got_grad_ref, *rest):
    outs, total = rest[:-1], rest[-1]
    total[...] = dot(own_ref[...], grad_ref[...], TN) + dot(
        got_ref[...], got_grad_ref[...], TN
    )
    rows = total.shape[0] // len(outs)
    for k, out in enumerate(outs):
        start = pl.multiple_of(rows * lax.rem(place_ref[0] + k, len(outs)), rows)
        out[...] = total[pl.ds(start, rows), :].astype(out.dtype)


def weight_part(place, own, got, grad, got_grad, interpret=False):
    count = SIZES[0]
    rows, width = own.shape[1] // count, grad.shape[1]
    return pl.pallas_call(
        weight_kernel,
        out_shape=tuple(
            jax.ShapeDtypeStruct((rows, width), jnp.bfloat16 if k else jnp.float32)
            for k in range(count)
        ),
        in_specs=[pl.BlockSpec(memory_space=pltpu.SMEM)]
        + [pl.BlockSpec(memory_space=pltpu.VMEM)] * 4,
        scratch_shapes=[pltpu.VMEM((own.shape[1], width), jnp.float32)],
        compiler_params=pltpu.CompilerParams(vmem_limit_bytes=32 << 20),
        interpret=interpret,
    )(place, own, got, grad, got_grad)


def exchange(values, axis):
    return lax.all_to_all(values, axis, split_axis=0, concat_axis=0, tiled=True)


def shift(values, axis, step, size):
    return lax.ppermute(values, axis, [(i, (i + step) % size) for i in range(size)])


def on_device(frame_tokens, visible, grad_output, norm_gain,
              query_weight, key_weight, value_weight, output_weight):
    low = jnp.bfloat16
    clips = lax.axis_size("dp")
    shards = SIZES[0] * SIZES[1] * SIZES[2]
    tokens = frame_tokens[0]
    frames, _, width = tokens.shape
    _, att = query_weight.shape
    me = lax.axis_index(PARTS)
    core = lax.axis_index("core")

    folded = jnp.concatenate(
        [output_weight[:, :width // 2], output_weight[:, width // 2:]], axis=0
    )
    share = jnp.concatenate(
        [
            jnp.concatenate([query_weight, key_weight], axis=1),
            jnp.concatenate([value_weight, folded], axis=1),
        ],
        axis=0,
    )
    line = exchange(jnp.broadcast_to(share[None], (SIZES[1],) + share.shape), "y")
    left, right = shift(line, "x", 1, SIZES[0]), shift(line, "x", -1, SIZES[0])
    far = shift(right, "x", -1, SIZES[0])
    pieces = (line, left, right, far)
    pieces += tuple(shift(piece, "core", 1, SIZES[2]) for piece in pieces)

    values = tokens.astype(jnp.float32)
    centered = values - jnp.mean(values, axis=-1, keepdims=True)
    inverse = lax.rsqrt(jnp.mean(centered * centered, axis=-1, keepdims=True) + NORM_EPS)
    scaled = centered * inverse
    normed = (scaled * norm_gain).astype(low)

    def to_cells(rows):
        sent = rows.transpose(1, 0, 2).reshape(shards, 2, -1)
        return exchange(sent, PARTS).reshape(shards * frames, -1)

    grad_cells = to_cells(grad_output[0])
    normed_cells = to_cells(normed)
    grad_got = shift(grad_cells, "core", 1, 2)
    cells = lax.dynamic_slice_in_dim(visible[0], me, 1, 1)[:, 0]

    per = att // shards
    column = jnp.arange(att, dtype=jnp.int32)
    x, y = column // (per * 16), column // (per * 2) % 8
    place = (x * 8 + y) * per + column % per
    side = column // per % 2
    at = place[:, None] == jnp.arange(att // 2, dtype=jnp.int32)[None, :]
    pick = jnp.stack(
        [at & (side == core)[:, None], at & (side != core)[:, None]]
    ).astype(low)

    spot = jnp.stack([lax.axis_index("x"), core]).astype(jnp.int32)
    sent, own, other, whole_out = cell_part(
        spot, normed_cells, grad_cells, cells, pieces, pick
    )
    got = shift(other, "core", 1, 2)
    back = exchange(sent.reshape(shards, 2, -1), PARTS)
    rows = back.reshape(shards, frames, att + width).transpose(1, 0, 2)
    mixed, grad_normed = rows[:, :, :att], rows[:, :, att:]

    slabs = weight_part(
        lax.axis_index("x").astype(jnp.int32)[None], own, got, grad_cells, grad_got
    )
    part = slabs[0]
    for k in range(1, SIZES[0]):
        part = part + shift(slabs[k], "x", k, SIZES[0]).astype(jnp.float32)
    part = part.astype(low).reshape(SIZES[1], 2, -1)
    part, _ = lax.optimization_barrier((part, back))
    part = jnp.sum(exchange(part, "y").astype(jnp.float32), axis=0).astype(low)
    part = exchange(jnp.broadcast_to(part[None], (clips,) + part.shape), "dp")
    grad_weight = jnp.sum(part.astype(jnp.float32), axis=0).reshape(per, width)

    flat_mixed = mixed.reshape(-1, att)
    update = jnp.dot(flat_mixed, whole_out, preferred_element_type=jnp.float32)
    block_rows = (values.reshape(-1, width) + update).astype(low).reshape(tokens.shape)
    weighted = grad_normed.astype(jnp.float32) * norm_gain
    first_mean = jnp.mean(weighted, axis=-1, keepdims=True)
    second_mean = jnp.mean(weighted * scaled, axis=-1, keepdims=True)
    grad_rows = inverse * (weighted - first_mean - scaled * second_mean)
    grad_rows = grad_rows + grad_output[0].astype(jnp.float32)
    return (block_rows[None], grad_rows.astype(low)[None], grad_weight)


def solution(mesh):
    fine = Mesh(mesh.devices.reshape(SIZES + (mesh.shape["dp"],)), PARTS + ("dp",))
    rows = P("dp", PARTS, None, None)
    weight = P(PARTS, None)
    return jax.shard_map(
        on_device,
        mesh=fine,
        in_specs=(rows, P("dp", None, None), rows, P(), weight, weight, weight, weight),
        out_specs=(rows, rows, weight),
        check_vma=False,
    )
```
